128 devices in a mesh: bin: 16 (over z_lo, x, core), trk: 8 (over y, z_hi).
Axes of the slice: x: 4, y: 4, z: 4 (z_hi: 2, z_lo: 2; z = z_hi * 2 + z_lo), core: 2. Of those that a mesh axis runs over, the one named last changes fastest.
Arguments:
- trunk: bfloat16 [8192, 1536], P(('bin', 'trk')), may hold values from -6 to 6
- norm_gain: float32 [1536], replicated, may hold values from 0.1 to 1.9
- w_query: bfloat16 [1536, 1024], replicated, may hold values from -0.4375 to 0.4375
- w_kv: bfloat16 [1536, 256], replicated, may hold values from -0.15625 to 0.15625
- w_out: bfloat16 [1024, 1536], replicated, may hold values from -0.1875 to 0.1875
- w_up: bfloat16 [1536, 768], replicated, may hold values from -0.15625 to 0.15625
- skip: bfloat16 [32768, 768], P(('bin', 'trk')), may hold values from -6 to 6
- conv_w: bfloat16 [5, 768, 768], replicated, may hold values from -0.09375 to 0.09375
- head_w: bfloat16 [768, 6144], P(None, 'trk'), may hold values from -0.21875 to 0.21875
- head_bias: float32 [6144], P('trk'), may hold values from -4 to 4
- targets: bfloat16 [32768, 6144], P('bin', 'trk'), may hold values from 0.049804688 to 4
- missing: int32 [8192], P('bin'), may hold values 0 or 1
- group_ids: int32 [6144, 1], replicated, may hold values from 0 to 10
- group_weight: float32 [11], replicated, may hold values from 0.25 to 4
Outputs:
- prediction: bfloat16 [32768, 6144], P('bin', 'trk')
- head_grad: float32 [768, 6144], P('bin', 'trk')
- feature_grad: bfloat16 [32768, 768], P(('bin', 'trk'))
The draws below stay inside these ranges and needn't reach their ends.
Inputs may be any that keep to these rules, and one draw needn't show every extreme that they name: `group_ids`: every group id is held by at least one track.
All inputs are finite; a program needn't handle non-finite values. No bound on the sum of `missing` on one device may be relied on, other than what follows from the above.
Results may differ from the reference program's by a relative error of at most 0.019.
Values may be sent and summed in bfloat16 or wider, within the bound.
No kernel may reach another device: no remote copies, remote signals or barrier semaphores. Data moves between devices by JAX's collectives and lax.ppermute only.
A program may use at most 128 MiB of HBM per device.

```python
import math
import jax
import jax.numpy as jnp
from jax import lax

C = 1536
HEADS = 8
DK = 128
C2 = 768
KW = 5
UP = 4
GROUPS = 11
TR_DEV = 768
NB = 8192
NP = 32768
TRACKS = 6144
N_TRK = 8


def place_ends(drawn, stream_key, least, high):
    shape = drawn.shape
    place = [jax.random.randint(jax.random.fold_in(stream_key, axis), (), 0, shape[axis]) for axis in range(len(shape))]
    drawn = drawn.at[tuple(place)].set(least)
    longest = shape.index(max(shape))
    place[longest] = (place[longest] + 1) % shape[longest]
    return drawn.at[tuple(place)].set(high)


def steps_of(rng, extent, shards, low, largest):
    level, own = 1.0, jax.random.fold_in(rng, 6)
    for axis_at, shards_of in shards:
        draws = jnp.exp(jax.random.uniform(jax.random.fold_in(own, axis_at), (shards_of,), jnp.float32, low / len(shards), largest / len(shards)))
        level = level * jnp.repeat(draws, extent[axis_at] // shards_of).reshape([-1 if axis == axis_at else 1 for axis in range(len(extent))])
    return level


def distinct(key, rows, amount, top, lift):
    sequence = jax.random.permutation(jax.random.fold_in(key, 1), amount)
    pull = sequence
    for power in range(3):
        pull = pull * pull // amount
    pull = pull * lift // amount
    lots = jax.random.randint(jax.random.fold_in(key, 2), (rows, amount), 0, 4096) + pull
    sure = jax.random.permutation(jax.random.fold_in(key, 3), rows)[jnp.arange(amount) % rows]
    lots = jnp.where(jnp.arange(rows)[:, None] == sure[None, :], 1 << 14, lots)
    score = lots * amount + jnp.arange(amount)
    return lax.top_k(score.astype(jnp.int32), top)[1].astype(jnp.int32)


def bell_draw(stream_key, extent, deviation, reach, pieces=(), kind=jnp.bfloat16):
    entries = jax.random.normal(stream_key, extent, jnp.float32) * deviation
    if len(pieces) > 0:
        entries = steps_of(stream_key, extent, pieces, -0.22, 0.18) * entries
    return jnp.clip(entries, min=-reach, max=reach).astype(kind)


def setup_inputs(seed: int = 0) -> dict:
    splits = jax.random.split(jax.random.key(seed), 15)
    trunk = bell_draw(splits[0], (NB, C), 1.0, 6.0, ((0, 128),))
    norm_gain = jnp.clip(1.0 + 0.18 * jax.random.normal(splits[1], (C,), jnp.float32), 0.1, 1.9)
    w_query = bell_draw(splits[2], (C, HEADS * DK), (C // 9) ** -0.5, 0.4375)
    w_kv = bell_draw(splits[3], (C, 2 * DK), C ** -0.5, 0.15625)
    w_out = bell_draw(splits[4], (HEADS * DK, C), (HEADS * DK) ** -0.5, 0.1875)
    w_up = bell_draw(splits[5], (C, C2), C ** -0.5, 0.15625)
    skip = bell_draw(splits[6], (NP, C2), 1.0, 6.0, ((0, 128),))
    conv_w = bell_draw(splits[7], (KW, C2, C2), (KW * C2) ** -0.5, 0.09375)
    head_w = bell_draw(splits[8], (C2, TRACKS), C2 ** -0.5, 0.21875, ((1, 8),))
    head_bias = bell_draw(splits[9], (TRACKS,), 1.0, 4.0, ((0, 8),), jnp.float32)
    targets = jnp.clip(jnp.exp(math.log(4.0) - 4.3859405 * jax.random.uniform(splits[10], (NP, TRACKS), jnp.float32) ** steps_of(splits[10], (NP, TRACKS), ((0, 16), (1, 8)), -0.2, 0.2)), 0.049804688, 4.0).astype(jnp.bfloat16)
    missing = place_ends((jax.random.randint(splits[11], (NB,), 0, 8) < 1).astype(jnp.int32), jax.random.fold_in(splits[11], 1), 0, 1)
    group_ids = distinct(splits[12], TRACKS, GROUPS, 1, 744)
    group_weight = jnp.clip(jnp.exp(jax.random.uniform(splits[13], (GROUPS,), jnp.float32, math.log(0.25), math.log(4.0))), 0.25, 4.0)
    return {"trunk": trunk, "norm_gain": norm_gain, "w_query": w_query, "w_kv": w_kv, "w_out": w_out, "w_up": w_up, "skip": skip, "conv_w": conv_w, "head_w": head_w, "head_bias": head_bias, "targets": targets, "missing": missing, "group_ids": group_ids, "group_weight": group_weight}


logit_cap = 20.0

def reference(trunk, norm_gain, w_query, w_kv, w_out, w_up, skip, conv_w, head_w, head_bias, targets, missing, group_ids, group_weight):
    widened = trunk.astype(jnp.float32)
    meansq = lax.optimization_barrier(jnp.mean(widened * widened, axis=1, keepdims=True))
    normed = (widened * lax.rsqrt(meansq + 1e-06) * norm_gain).astype(jnp.bfloat16)
    queries = jnp.dot(normed, w_query, preferred_element_type=jnp.float32).astype(jnp.bfloat16)
    keyvals = jnp.dot(normed, w_kv, preferred_element_type=jnp.float32).astype(jnp.bfloat16)
    key_rows = keyvals[:, :DK].astype(jnp.float32)
    value_rows = keyvals[:, DK:].astype(jnp.float32)
    block_rows = math.gcd(NB, 512)
    query_blocks = queries.reshape(NB // block_rows, block_rows, HEADS, DK)
    score_scale = 1.0 / math.sqrt(DK)

    def attend(query_block):
        scores = jnp.einsum('qhd,nd->qhn', query_block.astype(jnp.float32), key_rows) * score_scale
        scores = logit_cap * jnp.tanh(scores / logit_cap)
        exp_weights = jnp.exp(scores)
        denominator = lax.optimization_barrier(jnp.sum(exp_weights, axis=2))
        rounded = lax.optimization_barrier(exp_weights.astype(jnp.bfloat16)).astype(jnp.float32)
        numerator = jnp.einsum('qhn,nd->qhd', rounded, value_rows)
        return (numerator / denominator[:, :, None]).astype(jnp.bfloat16)
    attended = lax.map(attend, query_blocks).reshape(NB, HEADS * DK)
    hidden = (widened + jnp.dot(attended, w_out, preferred_element_type=jnp.float32)).astype(jnp.bfloat16)
    upward = jnp.dot(hidden, w_up, preferred_element_type=jnp.float32)
    upsampled = (jnp.repeat(upward, UP, axis=0) + skip.astype(jnp.float32)).astype(jnp.bfloat16)
    rim_width = KW // 2
    padded = jnp.pad(upsampled, ((rim_width, rim_width), (0, 0)))
    conved = jnp.zeros((NP, C2), jnp.float32)
    for tap in range(KW):
        conved = conved + jnp.dot(padded[tap:tap + NP], conv_w[tap], preferred_element_type=jnp.float32)
    feature = (upsampled.astype(jnp.float32) + jax.nn.gelu(conved)).astype(jnp.bfloat16)
    labels = jnp.arange(GROUPS, dtype=jnp.int32)
    member = group_ids == labels[None, :]
    counts = lax.optimization_barrier(jnp.sum(member.astype(jnp.int32), axis=0))
    per_group = group_weight * TRACKS / (GROUPS * counts.astype(jnp.float32))
    track_scale = lax.optimization_barrier(jnp.sum(jnp.where(member, per_group[None, :], 0.0), axis=1))
    keep_mask = 1.0 - jnp.repeat(missing.astype(jnp.float32), UP)[:, None]
    weight_tiles = head_w.reshape(C2, N_TRK, TR_DEV).transpose(1, 0, 2)
    bias_tiles = head_bias.reshape(N_TRK, TR_DEV)
    target_tiles = targets.reshape(NP, N_TRK, TR_DEV).transpose(1, 0, 2)
    scale_tiles = track_scale.reshape(N_TRK, TR_DEV)

    def head_tile(grad_sum, tile_data):
        tile_weight, tile_bias, tile_target, tile_scale = tile_data
        logits = jnp.dot(feature, tile_weight, preferred_element_type=jnp.float32) + tile_bias
        smooth = jax.nn.softplus(logits)
        misfit = smooth - tile_target.astype(jnp.float32)
        slope_grad = (keep_mask * tile_scale[None, :] * misfit * jax.nn.sigmoid(logits)).astype(jnp.bfloat16)
        weight_grad = jnp.dot(feature.T, slope_grad, preferred_element_type=jnp.float32) / NP
        partial_value = jnp.dot(slope_grad, tile_weight.T, preferred_element_type=jnp.float32)
        partial_value = lax.optimization_barrier(partial_value.astype(jnp.bfloat16)).astype(jnp.float32)
        return (grad_sum + partial_value, (smooth.astype(jnp.bfloat16), weight_grad))
    grad_sum, (pred_tiles, grad_tiles) = lax.scan(head_tile, jnp.zeros((NP, C2), jnp.float32), (weight_tiles, bias_tiles, target_tiles, scale_tiles))
    prediction = pred_tiles.transpose(1, 0, 2).reshape(NP, TRACKS)
    head_grad = grad_tiles.transpose(1, 0, 2).reshape(C2, TRACKS)
    return (prediction, head_grad, grad_sum.astype(jnp.bfloat16))
```

```python
import functools
import math

import jax
import jax.numpy as jnp
import numpy as np
from jax import lax
from jax.experimental import pallas as pl
from jax.experimental.pallas import tpu as pltpu
from jax.sharding import Mesh, PartitionSpec as P

logit_cap = 20.0
BIN = ("bz", "core")
TRK = ("y", "zh")
ALL = BIN + TRK


def place(index):
    bz, rest = divmod(index, 16)
    core, rest = divmod(rest, 8)
    y, zh = divmod(rest, 2)
    zlo, x = divmod(bz, 4)
    return (x, y, zh * 2 + zlo, core)


def number(x, y, z, core):
    zh, zlo = divmod(z, 2)
    return ((zlo * 4 + x) * 2 + core) * 8 + y * 2 + zh


def moved(value, dim, step):
    sizes = (4, 4, 4, 2)
    pairs = []
    for index in range(128):
        target = list(place(index))
        target[dim] = (target[dim] + step) % sizes[dim]
        pairs.append((index, number(*target)))
    return lax.ppermute(value, ALL, pairs)


def whole(array):
    return pl.BlockSpec(array.shape, lambda *_: (0,) * array.ndim, pipeline_mode=pl.Buffered(1))


def attend_kernel(head_dim, first, *refs):
    q_ref, refs = refs[0], refs[1:]
    num_ref, den_ref = refs[-2:]
    pieces = refs[:-2] if first else refs[:-4]
    f32, bf16 = jnp.float32, jnp.bfloat16
    heads = q_ref.shape[1] // head_dim
    queries = jnp.concatenate(
        [q_ref[:, h * head_dim : (h + 1) * head_dim] for h in range(heads)], 0
    )
    inner = 1.0 / (math.sqrt(head_dim) * logit_cap)
    outer = logit_cap * math.log2(math.e)
    num = jnp.zeros(num_ref.shape, f32) if first else refs[-4][...]
    den = jnp.zeros(den_ref.shape, f32) if first else refs[-3][...]
    step = 256
    for piece in pieces:
        for start in range(0, piece.shape[0], step):
            keys = piece[start : start + step, :head_dim]
            values = piece[start : start + step, head_dim:]
            scores = lax.dot_general(
                queries, keys, (((1,), (1,)), ((), ())), preferred_element_type=f32
            )
            weights = jnp.exp2(outer * jnp.tanh(scores * inner))
            num = num + jnp.dot(weights.astype(bf16), values, preferred_element_type=f32)
            for lane in range(0, step, 128):
                den = den + weights[:, lane : lane + 128]
    num_ref[...] = num
    den_ref[...] = den


def attend(state, queries, pieces, head_dim):
    rows = queries.shape[0] * queries.shape[1] // head_dim
    operands = [queries, *pieces, *(state or ())]
    keys = sum(piece.shape[0] for piece in pieces)
    return pl.pallas_call(
        functools.partial(attend_kernel, head_dim, state is None),
        grid=(1,),
        in_specs=[whole(operand) for operand in operands],
        out_specs=[pl.BlockSpec((rows, head_dim), lambda i: (0, 0))] * 2,
        out_shape=[jax.ShapeDtypeStruct((rows, head_dim), jnp.float32)] * 2,
        cost_estimate=pl.CostEstimate(
            flops=8 * rows * keys * head_dim,
            transcendentals=2 * rows * keys,
            bytes_accessed=1 << 20,
        ),
        compiler_params=pltpu.CompilerParams(vmem_limit_bytes=24 << 20),
        name="attend",
    )(*operands)


def project_kernel(num_ref, den_ref, trunk_ref, out_ref, up_ref, upward_ref):
    f32, bf16 = jnp.float32, jnp.bfloat16
    rows = trunk_ref.shape[0]
    total = jnp.sum(den_ref[...], axis=1, keepdims=True)
    ratio = (num_ref[...] / total).astype(bf16)
    heads = ratio.shape[0] // rows
    attended = jnp.concatenate([ratio[h * rows : (h + 1) * rows] for h in range(heads)], 1)
    hidden = (
        trunk_ref[...].astype(f32)
        + jnp.dot(attended, out_ref[...], preferred_element_type=f32)
    ).astype(bf16)
    upward_ref[...] = jnp.dot(hidden, up_ref[...], preferred_element_type=f32).astype(bf16)


def project(state, trunk, w_out, w_up):
    operands = (*state, trunk, w_out, w_up)
    out = jax.ShapeDtypeStruct((trunk.shape[0], w_up.shape[1]), jnp.bfloat16)
    return pl.pallas_call(
        project_kernel,
        grid=(1,),
        in_specs=[whole(operand) for operand in operands],
        out_specs=whole(out),
        out_shape=out,
        cost_estimate=pl.CostEstimate(
            flops=2 * trunk.shape[0] * (w_out.size + w_up.size),
            transcendentals=0,
            bytes_accessed=2 * (w_out.size + w_up.size),
        ),
        compiler_params=pltpu.CompilerParams(vmem_limit_bytes=24 << 20),
        name="project",
    )(*operands)


def head_kernel(
    positions, core_ref, up_ref, skip_ref, before_ref, after_ref, conv_ref, head_ref, bias_ref,
    scale_ref, keep_ref, target_ref, pred_ref, partial_ref, mine_ref, theirs_ref, wide, near, total,
):
    f32, bf16 = jnp.float32, jnp.bfloat16
    step = pl.program_id(0)
    rows, channels = pred_ref.shape[0], up_ref.shape[1]
    segments = skip_ref.shape[0] // rows
    bins = up_ref.shape[0] // segments
    factor = rows // bins
    taps = conv_ref.shape[0]
    rim = taps // 2

    @pl.when(step == 0)
    def _():
        wide[0:8, :] = jnp.zeros((8, channels), f32)
        wide[8 - rim : 8, :] = before_ref[...].astype(f32)
        wide[8 + segments * rows : 16 + segments * rows, :] = jnp.zeros((8, channels), f32)
        wide[8 + segments * rows : 8 + segments * rows + rim, :] = after_ref[...].astype(f32)
        row = lax.broadcasted_iota(jnp.int32, (rows, bins), 0)
        col = lax.broadcasted_iota(jnp.int32, (rows, bins), 1) * factor
        spread = jnp.where((row >= col) & (row < col + factor), 1.0, 0.0).astype(bf16)

        def expand(segment, carry):
            at = pl.multiple_of(segment * rows, rows)
            source = pl.multiple_of(segment * bins, bins)
            tall = jnp.dot(spread, up_ref[pl.ds(source, bins), :], preferred_element_type=f32)
            tall = (tall + skip_ref[pl.ds(at, rows), :].astype(f32)).astype(bf16)
            wide[pl.ds(at + 8, rows), :] = tall.astype(f32)
            return carry

        lax.fori_loop(0, segments, expand, 0)
        total[...] = jnp.zeros(total.shape, f32)

    near[...] = wide[pl.ds(pl.multiple_of(step * rows, rows), rows + 16), :]
    conved = jnp.zeros((rows, channels), f32)
    for tap in range(taps):
        begin = 8 - rim + tap
        conved = conved + jnp.dot(
            near[begin : begin + rows, :].astype(bf16), conv_ref[tap], preferred_element_type=f32
        )
    cubic = math.sqrt(2.0 / math.pi) * (conved + 0.044715 * (conved * conved * conved))
    feature = (near[8 : 8 + rows, :] + 0.5 * conved * (1.0 + jnp.tanh(cubic))).astype(bf16)
    logits = jnp.dot(feature, head_ref[...], preferred_element_type=f32) + bias_ref[...]
    decay = jnp.exp(-jnp.abs(logits))
    smooth = jnp.maximum(logits, 0.0) + jnp.log1p(decay)
    sigmoid = jnp.where(logits >= 0.0, 1.0, decay) / (1.0 + decay)
    pred_ref[...] = smooth.astype(bf16)
    misfit = smooth - target_ref[...].astype(f32)
    slope = (keep_ref[...] * scale_ref[...] * misfit * sigmoid).astype(bf16)
    partial_ref[...] = lax.dot_general(
        slope, head_ref[...], (((1,), (1,)), ((), ())), preferred_element_type=f32
    ).astype(bf16)
    total[...] += lax.dot_general(
        feature, slope, (((0,), (0,)), ((), ())), preferred_element_type=f32
    )

    @pl.when(step == segments - 1)
    def _():
        core = core_ref[0]
        pairs, height = 8, channels // 16
        for pair in range(pairs):
            at = pl.multiple_of((2 * pair + core) * height, height)
            other = pl.multiple_of((2 * pair + 1 - core) * height, height)
            into = slice(pair * height, (pair + 1) * height)
            mine_ref[into, :] = total[pl.ds(at, height), :] / positions
            theirs_ref[into, :] = (total[pl.ds(other, height), :] / positions).astype(bf16)


def head_pass(core, up, skip, before, after, conv_w, head_w, bias, scale, keep, targets, positions):
    f32, bf16 = jnp.float32, jnp.bfloat16
    count, channels = skip.shape
    segments = 8
    rows = count // segments
    tracks = head_w.shape[1]
    by_rows = pl.BlockSpec((rows, tracks), lambda i, core: (i, 0))
    operands = (up, skip, before, after, conv_w, head_w, bias, scale)
    half = (channels // 2, tracks)
    return pl.pallas_call(
        functools.partial(head_kernel, positions),
        grid_spec=pltpu.PrefetchScalarGridSpec(
            num_scalar_prefetch=1,
            grid=(segments,),
            in_specs=[whole(operand) for operand in operands]
            + [pl.BlockSpec((rows, 1), lambda i, core: (i, 0)), by_rows],
            out_specs=[
                by_rows,
                pl.BlockSpec((rows, channels), lambda i, core: (i, 0)),
                pl.BlockSpec(half, lambda i, core: (0, 0)),
                pl.BlockSpec(half, lambda i, core: (0, 0)),
            ],
            scratch_shapes=[
                pltpu.VMEM((count + 16, channels), f32),
                pltpu.VMEM((rows + 16, channels), f32),
                pltpu.VMEM((channels, tracks), f32),
            ],
        ),
        out_shape=[
            jax.ShapeDtypeStruct((count, tracks), bf16),
            jax.ShapeDtypeStruct((count, channels), bf16),
            jax.ShapeDtypeStruct(half, f32),
            jax.ShapeDtypeStruct(half, bf16),
        ],
        cost_estimate=pl.CostEstimate(
            flops=2 * count * (conv_w.size + 3 * head_w.size),
            transcendentals=4 * count * tracks,
            bytes_accessed=24 << 20,
        ),
        compiler_params=pltpu.CompilerParams(vmem_limit_bytes=44 << 20),
        name="head_pass",
    )(core, *operands, keep, targets)


def body(
    trunk,
    norm_gain,
    w_query,
    w_kv,
    w_out,
    w_up,
    skip,
    conv_w,
    head_w,
    head_bias,
    targets,
    missing,
    group_ids,
    group_weight,
):
    f32, bf16 = jnp.float32, jnp.bfloat16
    row_count = trunk.shape[0]
    head_dim = w_kv.shape[1] // 2
    head_count = w_query.shape[1] // head_dim
    skip_all = lax.all_gather(skip, TRK, axis=0, tiled=True)
    widened = trunk.astype(f32)
    meansq = jnp.mean(widened * widened, axis=1, keepdims=True)
    normed = (widened * lax.rsqrt(meansq + 1e-06) * norm_gain).astype(bf16)
    keyvals = jnp.dot(normed, w_kv, preferred_element_type=f32).astype(bf16)
    for dim in (2, 1):
        keyvals = jnp.concatenate([keyvals] + [moved(keyvals, dim, step) for step in (1, 3, 2)], 0)
    queries = jnp.dot(normed, w_query, preferred_element_type=f32).astype(bf16)
    crossed = moved(keyvals, 3, 1)
    pieces = [moved(keyvals, 0, step) for step in (1, 3, 2)]
    state = attend(None, queries, [keyvals], head_dim)
    for piece in pieces:
        state = attend(state, queries, [crossed, piece], head_dim)
        crossed = moved(piece, 3, 1)
    state = attend(state, queries, [crossed], head_dim)
    upward = project(state, trunk, w_out, w_up)
    n_trk = lax.axis_size(TRK)
    upward_all = lax.all_to_all(
        jnp.broadcast_to(upward[None], (n_trk,) + upward.shape), TRK, 0, 0, tiled=True
    ).reshape(n_trk * row_count, upward.shape[1])
    factor = skip.shape[0] // row_count
    tap_count, channels = conv_w.shape[:2]
    rim = tap_count // 2
    pos_count = skip_all.shape[0]
    n_bin = lax.axis_size(BIN)
    up_pairs = [(i, i + 1) for i in range(n_bin - 1)]
    last = upward_all[-1:].astype(f32) + skip_all[pos_count - rim :].astype(f32)
    first = upward_all[:1].astype(f32) + skip_all[:rim].astype(f32)
    before = lax.ppermute(last.astype(bf16), BIN, up_pairs)
    after = lax.ppermute(first.astype(bf16), BIN, [(j, i) for i, j in up_pairs])
    tile_width = head_w.shape[1]
    groups = group_weight.shape[0]
    total_tracks = group_ids.shape[0]
    labels = jnp.arange(groups, dtype=jnp.int32)
    counts = jnp.sum((group_ids == labels[None, :]).astype(jnp.int32), axis=0)
    per_group = group_weight * total_tracks / (groups * counts.astype(f32))
    local_ids = lax.dynamic_slice_in_dim(group_ids, lax.axis_index(TRK) * tile_width, tile_width, 0)
    track_scale = jnp.sum(jnp.where(local_ids == labels[None, :], per_group[None, :], 0.0), axis=1)
    keep_mask = 1.0 - jnp.repeat(missing.astype(f32), factor)[:, None]
    core = lax.axis_index("core")
    prediction, partial_value, mine, theirs = head_pass(
        core[None].astype(jnp.int32),
        upward_all,
        skip_all,
        before,
        after,
        conv_w,
        head_w,
        head_bias[None, :],
        track_scale[None, :],
        keep_mask,
        targets,
        pos_count * n_bin,
    )
    arrived = lax.all_to_all(
        partial_value.reshape(n_trk, pos_count // n_trk, channels), TRK, 0, 0, tiled=True
    )
    feature_grad = jnp.sum(arrived.astype(f32), axis=0).astype(bf16)
    pair_sum = (mine + lax.ppermute(theirs, "core", [(0, 1), (1, 0)]).astype(f32)).astype(bf16)
    pair_sum = pair_sum.reshape(lax.axis_size("bz"), channels // n_bin, tile_width)
    gathered = lax.all_to_all(pair_sum, "bz", 0, 0, tiled=True)
    head_grad = jnp.sum(gathered.astype(f32), axis=0)
    return (prediction, head_grad, feature_grad)


def solution(mesh):
    inner = Mesh(np.asarray(mesh.devices).reshape(8, 2, 4, 2), ALL)
    in_specs = (
        P(ALL, None),
        P(),
        P(),
        P(),
        P(),
        P(),
        P(ALL, None),
        P(),
        P(None, TRK),
        P(TRK),
        P(BIN, TRK),
        P(BIN),
        P(),
        P(),
    )
    out_specs = (P(BIN, TRK), P(BIN, TRK), P(ALL, None))
    return jax.shard_map(body, mesh=inner, in_specs=in_specs, out_specs=out_specs, check_vma=False)
```

```python
import functools
import math

import jax
import jax.numpy as jnp
import numpy as np
from jax import lax
from jax.experimental import pallas as pl
from jax.experimental.pallas import tpu as pltpu
from jax.sharding import Mesh, PartitionSpec as P

logit_cap = 20.0
PARTS = 2
BIN = ("bz", "core")
TRK = ("y", "zh")
ALL = BIN + TRK


def place(index):
    bz, rest = divmod(index, 16)
    core, rest = divmod(rest, 8)
    y, zh = divmod(rest, 2)
    zlo, x = divmod(bz, 4)
    return (x, y, zh * 2 + zlo, core)


def number(x, y, z, core):
    zh, zlo = divmod(z, 2)
    return ((zlo * 4 + x) * 2 + core) * 8 + y * 2 + zh


def moved(value, dim, step):
    sizes = (4, 4, 4, 2)
    pairs = []
    for index in range(128):
        target = list(place(index))
        target[dim] = (target[dim] + step) % sizes[dim]
        pairs.append((index, number(*target)))
    return lax.ppermute(value, ALL, pairs)


def whole(array):
    return pl.BlockSpec(array.shape, lambda *_: (0,) * array.ndim, pipeline_mode=pl.Buffered(1))


def attend_kernel(head_dim, first, *refs):
    q_ref, refs = refs[0], refs[1:]
    num_ref, den_ref = refs[-2:]
    pieces = refs[:-2] if first else refs[:-4]
    f32, bf16 = jnp.float32, jnp.bfloat16
    heads = q_ref.shape[1] // head_dim
    queries = jnp.concatenate(
        [q_ref[:, h * head_dim : (h + 1) * head_dim] for h in range(heads)], 0
    )
    inner = 1.0 / (math.sqrt(head_dim) * logit_cap)
    outer = logit_cap * math.log2(math.e)
    num = jnp.zeros(num_ref.shape, f32) if first else refs[-4][...]
    den = jnp.zeros(den_ref.shape, f32) if first else refs[-3][...]
    step = 512
    for piece in pieces:

        def block(index, pair, piece=piece):
            num, den = pair
            rows = pl.ds(pl.multiple_of(index * step, step), step)
            scores = lax.dot_general(
                queries, piece[rows, :head_dim], (((1,), (1,)), ((), ())), preferred_element_type=f32
            )
            weights = jnp.exp2(outer * jnp.tanh(scores * inner))
            num = num + jnp.dot(
                weights.astype(bf16), piece[rows, head_dim:], preferred_element_type=f32
            )
            for lane in range(0, step, 128):
                den = den + weights[:, lane : lane + 128]
            return num, den

        num, den = lax.fori_loop(0, piece.shape[0] // step, block, (num, den))
    num_ref[...] = num
    den_ref[...] = den


def attend(state, queries, pieces, head_dim):
    rows = queries.shape[0] * queries.shape[1] // head_dim
    operands = [queries, *pieces, *(state or ())]
    keys = sum(piece.shape[0] for piece in pieces)
    return pl.pallas_call(
        functools.partial(attend_kernel, head_dim, state is None),
        grid=(1,),
        in_specs=[whole(operand) for operand in operands],
        out_specs=[pl.BlockSpec((rows, head_dim), lambda i: (0, 0))] * 2,
        out_shape=[jax.ShapeDtypeStruct((rows, head_dim), jnp.float32)] * 2,
        cost_estimate=pl.CostEstimate(
            flops=8 * rows * keys * head_dim,
            transcendentals=2 * rows * keys,
            bytes_accessed=1 << 20,
        ),
        compiler_params=pltpu.CompilerParams(vmem_limit_bytes=24 << 20),
        name="attend",
    )(*operands)


def project_kernel(num_ref, den_ref, trunk_ref, out_ref, up_ref, upward_ref):
    f32, bf16 = jnp.float32, jnp.bfloat16
    rows = trunk_ref.shape[0]
    total = jnp.sum(den_ref[...], axis=1, keepdims=True)
    ratio = (num_ref[...] / total).astype(bf16)
    heads = ratio.shape[0] // rows
    attended = jnp.concatenate([ratio[h * rows : (h + 1) * rows] for h in range(heads)], 1)
    hidden = (
        trunk_ref[...].astype(f32)
        + jnp.dot(attended, out_ref[...], preferred_element_type=f32)
    ).astype(bf16)
    upward_ref[...] = jnp.dot(hidden, up_ref[...], preferred_element_type=f32).astype(bf16)


def project(state, trunk, w_out, w_up):
    operands = (*state, trunk, w_out, w_up)
    out = jax.ShapeDtypeStruct((trunk.shape[0], w_up.shape[1]), jnp.bfloat16)
    return pl.pallas_call(
        project_kernel,
        grid=(1,),
        in_specs=[whole(operand) for operand in operands],
        out_specs=whole(out),
        out_shape=out,
        cost_estimate=pl.CostEstimate(
            flops=2 * trunk.shape[0] * (w_out.size + w_up.size),
            transcendentals=0,
            bytes_accessed=2 * (w_out.size + w_up.size),
        ),
        compiler_params=pltpu.CompilerParams(vmem_limit_bytes=24 << 20),
        name="project",
    )(*operands)


def expand_kernel(at_ref, *refs):
    f32, bf16 = jnp.float32, jnp.bfloat16
    ups, skips, wide = refs[:4], refs[4:8], refs[8]
    bins, channels = ups[0].shape[0] // 2, ups[0].shape[1]
    rows = skips[0].shape[0] // 2
    factor = rows // bins
    row = lax.broadcasted_iota(jnp.int32, (rows, bins), 0)
    col = lax.broadcasted_iota(jnp.int32, (rows, bins), 1) * factor
    spread = jnp.where((row >= col) & (row < col + factor), 1.0, 0.0).astype(bf16)
    wide[0:8, :] = jnp.zeros((8, channels), f32)
    wide[8 * rows + 8 : 8 * rows + 16, :] = jnp.zeros((8, channels), f32)
    y, zh = at_ref[0], at_ref[1]
    for step in range(4):
        for half in range(2):
            other = zh if half == 0 else 1 - zh
            segment = 2 * lax.rem(y + 4 - step, 4) + other
            tall = jnp.dot(
                spread, ups[step][half * bins : (half + 1) * bins, :], preferred_element_type=f32
            )
            tall = tall + skips[step][half * rows : (half + 1) * rows, :].astype(f32)
            start = pl.multiple_of(segment * rows + 8, 8)
            wide[pl.ds(start, rows), :] = tall.astype(bf16).astype(f32)


def expand(at, ups, skips):
    operands = (*ups, *skips)
    channels = skips[0].shape[1]
    out = jax.ShapeDtypeStruct((4 * skips[0].shape[0] + 16, channels), jnp.float32)
    return pl.pallas_call(
        expand_kernel,
        grid_spec=pltpu.PrefetchScalarGridSpec(
            num_scalar_prefetch=1,
            grid=(1,),
            in_specs=[whole(operand) for operand in operands],
            out_specs=whole(out),
        ),
        out_shape=out,
        cost_estimate=pl.CostEstimate(
            flops=2 * out.size * 64, transcendentals=0, bytes_accessed=10 << 20
        ),
        compiler_params=pltpu.CompilerParams(vmem_limit_bytes=24 << 20),
        name="expand",
    )(at, *operands)


def head_kernel(
    first, last, positions, at_ref, wide_ref, before_ref, after_ref, conv_ref, head_ref, bias_ref,
    scale_ref, keep_ref, target_ref, *refs,
):
    f32, bf16 = jnp.float32, jnp.bfloat16
    if first:
        near, total = refs[-1], None
        pred_ref, partial_ref, total_ref = refs[:3]
    else:
        near, old_ref = refs[-1], refs[1]
        pred_ref, partial_ref, total_ref = refs[2:5]
    part = pl.program_id(0)
    segment = at_ref[0] * PARTS + part
    rows, channels = partial_ref.shape
    taps = conv_ref.shape[0]
    rim = taps // 2
    near[...] = wide_ref[pl.ds(pl.multiple_of(segment * rows, rows), rows + 16), :]

    @pl.when(segment == 0)
    def _():
        near[8 - rim : 8, :] = before_ref[...].astype(f32)

    @pl.when(segment == 4 * PARTS - 1)
    def _():
        near[rows + 8 : rows + 8 + rim, :] = after_ref[...].astype(f32)

    conved = jnp.zeros((rows, channels), f32)
    for tap in range(taps):
        begin = 8 - rim + tap
        conved = conved + jnp.dot(
            near[begin : begin + rows, :].astype(bf16), conv_ref[tap], preferred_element_type=f32
        )
    cubic = math.sqrt(2.0 / math.pi) * (conved + 0.044715 * (conved * conved * conved))
    feature = (near[8 : 8 + rows, :] + 0.5 * conved * (1.0 + jnp.tanh(cubic))).astype(bf16)
    logits = jnp.dot(feature, head_ref[...], preferred_element_type=f32) + bias_ref[...]
    decay = jnp.exp(-jnp.abs(logits))
    smooth = jnp.maximum(logits, 0.0) + jnp.log1p(decay)
    sigmoid = jnp.where(logits >= 0.0, 1.0, decay) / (1.0 + decay)
    pred_ref[...] = smooth.astype(bf16)
    misfit = smooth - target_ref[...].astype(f32)
    slope = (keep_ref[...] * scale_ref[...] * misfit * sigmoid).astype(bf16)
    partial_ref[...] = lax.dot_general(
        slope, head_ref[...], (((1,), (1,)), ((), ())), preferred_element_type=f32
    ).astype(bf16)
    product = lax.dot_general(
        feature, slope, (((0,), (0,)), ((), ())), preferred_element_type=f32
    )
    scale = 1.0 / positions if last else 1.0

    @pl.when(part == 0)
    def _():
        total_ref[...] = product if first else product + old_ref[...]

    @pl.when(part > 0)
    def _():
        total_ref[...] = (total_ref[...] + product) * scale


def head_pass(at, carried, wide, before, after, conv_w, head_w, bias, scale, keep, targets, last, positions):
    f32, bf16 = jnp.float32, jnp.bfloat16
    count, tracks = targets.shape
    channels = head_w.shape[0]
    rows = count // (4 * PARTS)
    first = carried is None
    by_rows = pl.BlockSpec((rows, tracks), lambda i, at: (at[0] * PARTS + i, 0))
    operands = (wide, before, after, conv_w, head_w, bias, scale)
    totals = jax.ShapeDtypeStruct((channels, tracks), f32)
    extra = [] if first else [pl.BlockSpec(memory_space=pl.ANY), whole(totals)]
    at_input = 1 + len(operands) + 2
    return pl.pallas_call(
        functools.partial(head_kernel, first, last, positions),
        grid_spec=pltpu.PrefetchScalarGridSpec(
            num_scalar_prefetch=1,
            grid=(PARTS,),
            in_specs=[whole(operand) for operand in operands]
            + [pl.BlockSpec((rows, 1), lambda i, at: (at[0] * PARTS + i, 0)), by_rows]
            + extra,
            out_specs=[by_rows, pl.BlockSpec((rows, channels), lambda i, at: (i, 0)), whole(totals)],
            scratch_shapes=[pltpu.VMEM((rows + 16, channels), f32)],
        ),
        out_shape=[
            jax.ShapeDtypeStruct((count, tracks), bf16),
            jax.ShapeDtypeStruct((PARTS * rows, channels), bf16),
            totals,
        ],
        input_output_aliases={} if first else {at_input: 0, at_input + 1: 2},
        cost_estimate=pl.CostEstimate(
            flops=2 * PARTS * rows * (conv_w.size + 3 * head_w.size),
            transcendentals=4 * PARTS * rows * tracks,
            bytes_accessed=16 << 20,
        ),
        compiler_params=pltpu.CompilerParams(vmem_limit_bytes=36 << 20),
        name="head_pass",
    )(at, *operands, keep, targets, *(carried or ()))


def body(
    trunk,
    norm_gain,
    w_query,
    w_kv,
    w_out,
    w_up,
    skip,
    conv_w,
    head_w,
    head_bias,
    targets,
    missing,
    group_ids,
    group_weight,
):
    f32, bf16 = jnp.float32, jnp.bfloat16
    row_count = trunk.shape[0]
    head_dim = w_kv.shape[1] // 2
    head_count = w_query.shape[1] // head_dim
    widened = trunk.astype(f32)
    meansq = jnp.mean(widened * widened, axis=1, keepdims=True)
    normed = (widened * lax.rsqrt(meansq + 1e-06) * norm_gain).astype(bf16)
    keyvals = jnp.dot(normed, w_kv, preferred_element_type=f32).astype(bf16)
    skip_pair = jnp.concatenate([skip, moved(skip, 2, 2)], 0)
    for dim in (2, 1):
        keyvals = jnp.concatenate([keyvals] + [moved(keyvals, dim, step) for step in (1, 3, 2)], 0)
    skip_pair, keyvals = lax.optimization_barrier((skip_pair, keyvals))
    queries = jnp.dot(normed, w_query, preferred_element_type=f32).astype(bf16)
    crossed = moved(keyvals, 3, 1)
    pieces = [moved(keyvals, 0, step) for step in (1, 3, 2)]
    skips = [skip_pair] + [moved(skip_pair, 1, step) for step in (1, 2, 3)]
    state = attend(None, queries, [keyvals], head_dim)
    for piece in pieces:
        state = attend(state, queries, [crossed, piece], head_dim)
        crossed = moved(piece, 3, 1)
    state = attend(state, queries, [crossed], head_dim)
    upward = project(state, trunk, w_out, w_up)
    up_pair = jnp.concatenate([upward, moved(upward, 2, 2)], 0)
    ups = [up_pair] + [moved(up_pair, 1, step) for step in (1, 2, 3)]
    y, zh, core = lax.axis_index("y"), lax.axis_index("zh"), lax.axis_index("core")
    wide = expand(jnp.stack([y, zh]).astype(jnp.int32), ups, skips)
    factor = skip.shape[0] // row_count
    tap_count, channels = conv_w.shape[:2]
    rim = tap_count // 2
    pos_count = targets.shape[0]
    n_bin = lax.axis_size(BIN)
    up_pairs = [(i, i + 1) for i in range(n_bin - 1)]
    before = lax.ppermute(wide[pos_count + 8 - rim : pos_count + 8].astype(bf16), BIN, up_pairs)
    after = lax.ppermute(wide[8 : 8 + rim].astype(bf16), BIN, [(j, i) for i, j in up_pairs])
    tile_width = head_w.shape[1]
    groups = group_weight.shape[0]
    total_tracks = group_ids.shape[0]
    labels = jnp.arange(groups, dtype=jnp.int32)
    counts = jnp.sum((group_ids == labels[None, :]).astype(jnp.int32), axis=0)
    per_group = group_weight * total_tracks / (groups * counts.astype(f32))
    local_ids = lax.dynamic_slice_in_dim(group_ids, lax.axis_index(TRK) * tile_width, tile_width, 0)
    track_scale = jnp.sum(jnp.where(local_ids == labels[None, :], per_group[None, :], 0.0), axis=1)
    keep_mask = 1.0 - jnp.repeat(missing.astype(f32), factor)[:, None]
    carried, received = None, []
    for step in (2, 1, 3, 0):
        prediction, partial, total = head_pass(
            jnp.stack([lax.rem(y + step, 4), core]).astype(jnp.int32),
            carried,
            wide,
            before,
            after,
            conv_w,
            head_w,
            head_bias[None, :],
            track_scale[None, :],
            keep_mask,
            targets,
            step == 0,
            pos_count * n_bin,
        )
        carried = (prediction, total)
        received.append(moved(partial, 1, step) if step else partial)
    summed = sum(part.astype(f32) for part in received)
    halves = summed.reshape(2, summed.shape[0] // 2, channels)
    away = lax.dynamic_index_in_dim(halves, 1 - zh, 0, keepdims=False).astype(bf16)
    here = lax.dynamic_index_in_dim(halves, zh, 0, keepdims=False)
    feature_grad = (here + moved(away, 2, 2).astype(f32)).astype(bf16)
    blocks = total.reshape(lax.axis_size("bz"), 2, channels // n_bin, tile_width)
    mine = lax.dynamic_index_in_dim(blocks, core, 1, keepdims=False)
    theirs = lax.dynamic_index_in_dim(blocks, 1 - core, 1, keepdims=False).astype(bf16)
    pair_sum = (mine + lax.ppermute(theirs, "core", [(0, 1), (1, 0)]).astype(f32)).astype(bf16)
    gathered = lax.all_to_all(pair_sum, "bz", 0, 0, tiled=True)
    head_grad = jnp.sum(gathered.astype(f32), axis=0)
    return (prediction, head_grad, feature_grad)


def solution(mesh):
    inner = Mesh(np.asarray(mesh.devices).reshape(8, 2, 4, 2), ALL)
    in_specs = (
        P(ALL, None),
        P(),
        P(),
        P(),
        P(),
        P(),
        P(ALL, None),
        P(),
        P(None, TRK),
        P(TRK),
        P(BIN, TRK),
        P(BIN),
        P(),
        P(),
    )
    out_specs = (P(BIN, TRK), P(BIN, TRK), P(ALL, None))
    return jax.shard_map(body, mesh=inner, in_specs=in_specs, out_specs=out_specs, check_vma=False)
```

```python
import functools
import math

import jax
import jax.numpy as jnp
import numpy as np
from jax import lax
from jax.experimental import pallas as pl
from jax.experimental.pallas import tpu as pltpu
from jax.sharding import Mesh, PartitionSpec as P

logit_cap = 20.0
PARTS = 2
HEADV = 20
BIN = ("bz", "core")
TRK = ("y", "zh")
ALL = BIN + TRK


def place(index):
    bz, rest = divmod(index, 16)
    core, rest = divmod(rest, 8)
    y, zh = divmod(rest, 2)
    zlo, x = divmod(bz, 4)
    return (x, y, zh * 2 + zlo, core)


def number(x, y, z, core):
    zh, zlo = divmod(z, 2)
    return ((zlo * 4 + x) * 2 + core) * 8 + y * 2 + zh


def moved(value, dim, step):
    sizes = (4, 4, 4, 2)
    pairs = []
    for index in range(128):
        target = list(place(index))
        target[dim] = (target[dim] + step) % sizes[dim]
        pairs.append((index, number(*target)))
    return lax.ppermute(value, ALL, pairs)


def whole(array):
    return pl.BlockSpec(array.shape, lambda *_: (0,) * array.ndim, pipeline_mode=pl.Buffered(1))


def join_kernel(*refs):
    out = refs[-1]
    rows = refs[0].shape[0]
    for index, ref in enumerate(refs[:-1]):
        out[index * rows : (index + 1) * rows, :] = ref[...]


def join(*pieces):
    rows, columns = pieces[0].shape
    out = jax.ShapeDtypeStruct((len(pieces) * rows, columns), pieces[0].dtype)
    return pl.pallas_call(
        join_kernel,
        in_specs=[pl.BlockSpec(memory_space=pltpu.VMEM)] * len(pieces),
        out_specs=pl.BlockSpec(memory_space=pltpu.VMEM),
        out_shape=out,
        cost_estimate=pl.CostEstimate(flops=0, transcendentals=0, bytes_accessed=4 * out.size),
        compiler_params=pltpu.CompilerParams(vmem_limit_bytes=4 << 20),
        name="join",
    )(*pieces)


def attend_kernel(head_dim, first, *refs):
    q_ref, refs = refs[0], refs[1:]
    num_ref, den_ref = refs[-2:]
    pieces = refs[:-2] if first else refs[:-4]
    f32, bf16 = jnp.float32, jnp.bfloat16
    heads = q_ref.shape[1] // head_dim
    queries = jnp.concatenate(
        [q_ref[:, h * head_dim : (h + 1) * head_dim] for h in range(heads)], 0
    )
    inner = 1.0 / (math.sqrt(head_dim) * logit_cap)
    outer = logit_cap * math.log2(math.e)
    num = jnp.zeros(num_ref.shape, f32) if first else refs[-4][...]
    den = jnp.zeros(den_ref.shape, f32) if first else refs[-3][...]
    step = 256
    for piece in pieces:
        for start in range(0, piece.shape[0], step):
            keys = piece[start : start + step, :head_dim]
            values = piece[start : start + step, head_dim:]
            scores = lax.dot_general(
                queries, keys, (((1,), (1,)), ((), ())), preferred_element_type=f32
            )
            weights = jnp.exp2(outer * jnp.tanh(scores * inner))
            num = num + jnp.dot(weights.astype(bf16), values, preferred_element_type=f32)
            for lane in range(0, step, 128):
                den = den + weights[:, lane : lane + 128]
    num_ref[...] = num
    den_ref[...] = den


def attend(state, queries, pieces, head_dim):
    rows = queries.shape[0] * queries.shape[1] // head_dim
    operands = [queries, *pieces, *(state or ())]
    keys = sum(piece.shape[0] for piece in pieces)
    return pl.pallas_call(
        functools.partial(attend_kernel, head_dim, state is None),
        grid=(1,),
        in_specs=[whole(operand) for operand in operands],
        out_specs=[pl.BlockSpec((rows, head_dim), lambda i: (0, 0))] * 2,
        out_shape=[jax.ShapeDtypeStruct((rows, head_dim), jnp.float32)] * 2,
        cost_estimate=pl.CostEstimate(
            flops=8 * rows * keys * head_dim,
            transcendentals=2 * rows * keys,
            bytes_accessed=1 << 20,
        ),
        compiler_params=pltpu.CompilerParams(vmem_limit_bytes=24 << 20),
        name="attend",
    )(*operands)


def project_kernel(num_ref, den_ref, trunk_ref, out_ref, up_ref, upward_ref):
    f32, bf16 = jnp.float32, jnp.bfloat16
    rows = trunk_ref.shape[0]
    total = jnp.sum(den_ref[...], axis=1, keepdims=True)
    ratio = (num_ref[...] / total).astype(bf16)
    heads = ratio.shape[0] // rows
    attended = jnp.concatenate([ratio[h * rows : (h + 1) * rows] for h in range(heads)], 1)
    hidden = (
        trunk_ref[...].astype(f32)
        + jnp.dot(attended, out_ref[...], preferred_element_type=f32)
    ).astype(bf16)
    upward_ref[...] = jnp.dot(hidden, up_ref[...], preferred_element_type=f32).astype(bf16)


def project(state, trunk, w_out, w_up):
    operands = (*state, trunk, w_out, w_up)
    out = jax.ShapeDtypeStruct((trunk.shape[0], w_up.shape[1]), jnp.bfloat16)
    return pl.pallas_call(
        project_kernel,
        grid=(1,),
        in_specs=[whole(operand) for operand in operands],
        out_specs=whole(out),
        out_shape=out,
        cost_estimate=pl.CostEstimate(
            flops=2 * trunk.shape[0] * (w_out.size + w_up.size),
            transcendentals=0,
            bytes_accessed=2 * (w_out.size + w_up.size),
        ),
        compiler_params=pltpu.CompilerParams(vmem_limit_bytes=24 << 20),
        name="project",
    )(*operands)


def expand_kernel(at_ref, *refs):
    f32, bf16 = jnp.float32, jnp.bfloat16
    ups, skips, (wide, first, last) = refs[:4], refs[4:6], refs[6:]
    bins, channels = ups[0].shape[0] // 2, ups[0].shape[1]
    rows = skips[0].shape[0] // 4
    factor = rows // bins
    row = lax.broadcasted_iota(jnp.int32, (rows, bins), 0)
    col = lax.broadcasted_iota(jnp.int32, (rows, bins), 1) * factor
    spread = jnp.where((row >= col) & (row < col + factor), 1.0, 0.0).astype(bf16)
    wide[0:8, :] = jnp.zeros((8, channels), f32)
    wide[8 * rows + 8 : 8 * rows + 16, :] = jnp.zeros((8, channels), f32)
    y, zh = at_ref[0], at_ref[1]
    for step in range(4):
        for half in range(2):
            other = zh if half == 0 else 1 - zh
            segment = 2 * lax.rem(y + 4 - step, 4) + other
            tall = jnp.dot(
                spread, ups[step][half * bins : (half + 1) * bins, :], preferred_element_type=f32
            )
            tall = tall + skips[half][step * rows : (step + 1) * rows, :].astype(f32)
            start = pl.multiple_of(segment * rows + 8, 8)
            wide[pl.ds(start, rows), :] = tall.astype(bf16).astype(f32)
    first[...] = wide[8:16, :].astype(bf16)
    last[...] = wide[8 * rows : 8 * rows + 8, :].astype(bf16)


def expand(at, ups, skips):
    operands = (*ups, *skips)
    channels = skips[0].shape[1]
    out = jax.ShapeDtypeStruct((2 * skips[0].shape[0] + 16, channels), jnp.float32)
    edge = jax.ShapeDtypeStruct((8, channels), jnp.bfloat16)
    return pl.pallas_call(
        expand_kernel,
        grid_spec=pltpu.PrefetchScalarGridSpec(
            num_scalar_prefetch=1,
            grid=(1,),
            in_specs=[pl.BlockSpec(memory_space=pltpu.VMEM)] * len(operands),
            out_specs=[pl.BlockSpec(memory_space=pltpu.VMEM)] * 3,
        ),
        out_shape=[out, edge, edge],
        cost_estimate=pl.CostEstimate(
            flops=2 * out.size * 64, transcendentals=0, bytes_accessed=10 << 20
        ),
        compiler_params=pltpu.CompilerParams(vmem_limit_bytes=8 << 20),
        name="expand",
    )(at, *operands)


def head_kernel(
    first, last, positions, at_ref, wide_ref, before_ref, after_ref, conv_ref, head_ref, bias_ref,
    scale_ref, keep_ref, target_ref, *refs,
):
    f32, bf16 = jnp.float32, jnp.bfloat16
    near = refs[-1]
    if first:
        pred_ref, partial_ref, total_ref = refs[:3]
    elif last:
        old_ref, pred_ref, partial_ref, mine_ref, theirs_ref, total_ref = refs[1:7]
    else:
        old_ref, pred_ref, partial_ref, total_ref = refs[1:5]
    part = pl.program_id(0)
    segment = at_ref[0] * PARTS + part
    rows, channels = partial_ref.shape
    taps = conv_ref.shape[0]
    rim = taps // 2
    near[...] = wide_ref[pl.ds(pl.multiple_of(segment * rows, rows), rows + 16), :]

    @pl.when(segment == 0)
    def _():
        near[0:8, :] = before_ref[...].astype(f32)

    @pl.when(segment == 4 * PARTS - 1)
    def _():
        near[rows + 8 : rows + 16, :] = after_ref[...].astype(f32)

    bins = keep_ref.shape[2]
    factor = PARTS * rows // bins
    row = lax.broadcasted_iota(jnp.int32, (rows, bins), 0) + part * rows
    col = lax.broadcasted_iota(jnp.int32, (rows, bins), 1) * factor
    spread = jnp.where((row >= col) & (row < col + factor), 1.0, 0.0).astype(bf16)
    keep = lax.dot_general(
        spread,
        jnp.broadcast_to(keep_ref[0].astype(bf16), (8, bins)),
        (((1,), (1,)), ((), ())),
        preferred_element_type=f32,
    )[:, :1]
    conved = jnp.zeros((rows, channels), f32)
    for tap in range(taps):
        begin = 8 - rim + tap
        conved = conved + jnp.dot(
            near[begin : begin + rows, :].astype(bf16), conv_ref[tap], preferred_element_type=f32
        )
    cubic = math.sqrt(2.0 / math.pi) * (conved + 0.044715 * (conved * conved * conved))
    feature = (near[8 : 8 + rows, :] + 0.5 * conved * (1.0 + jnp.tanh(cubic))).astype(bf16)
    logits = jnp.dot(feature, head_ref[...], preferred_element_type=f32) + bias_ref[...]
    decay = jnp.exp(-jnp.abs(logits))
    smooth = jnp.maximum(logits, 0.0) + jnp.log1p(decay)
    sigmoid = jnp.where(logits >= 0.0, 1.0, decay) / (1.0 + decay)
    pred_ref[...] = smooth.astype(bf16)
    misfit = smooth - target_ref[...].astype(f32)
    slope = (keep * scale_ref[...] * misfit * sigmoid).astype(bf16)
    partial_ref[...] = lax.dot_general(
        slope, head_ref[...], (((1,), (1,)), ((), ())), preferred_element_type=f32
    ).astype(bf16)
    product = lax.dot_general(
        feature, slope, (((0,), (0,)), ((), ())), preferred_element_type=f32
    )

    @pl.when(part == 0)
    def _():
        total_ref[...] = product if first else product + old_ref[...]

    @pl.when(part > 0)
    def _():
        if not last:
            total_ref[...] += product
            return
        total_ref[...] = (total_ref[...] + product) / positions
        core, height = at_ref[1], channels // 16
        for pair in range(8):
            at = pl.multiple_of((2 * pair + core) * height, height)
            other = pl.multiple_of((2 * pair + 1 - core) * height, height)
            into = slice(pair * height, (pair + 1) * height)
            mine_ref[into, :] = total_ref[pl.ds(at, height), :]
            theirs_ref[into, :] = total_ref[pl.ds(other, height), :].astype(bf16)


def head_pass(at, carried, wide, before, after, conv_w, head_w, bias, scale, keep, targets, last, positions):
    f32, bf16 = jnp.float32, jnp.bfloat16
    count, tracks = targets.shape
    channels = head_w.shape[0]
    rows = count // (4 * PARTS)
    first = carried is None
    by_rows = pl.BlockSpec((rows, tracks), lambda i, at: (at[0] * PARTS + i, 0))
    operands = (wide, before, after, conv_w, head_w, bias, scale)
    totals = jax.ShapeDtypeStruct((channels, tracks), f32)
    extra = [] if first else [pl.BlockSpec(memory_space=pl.ANY), pl.BlockSpec(memory_space=pltpu.VMEM)]
    at_input = 1 + len(operands) + 2
    half = (channels // 2, tracks)
    sums = [jax.ShapeDtypeStruct(half, f32), jax.ShapeDtypeStruct(half, bf16)] if last else [totals]
    return pl.pallas_call(
        functools.partial(head_kernel, first, last, positions),
        grid_spec=pltpu.PrefetchScalarGridSpec(
            num_scalar_prefetch=1,
            grid=(PARTS,),
            in_specs=[pl.BlockSpec(memory_space=pltpu.VMEM)] * len(operands)
            + [pl.BlockSpec((1,) + keep.shape[1:], lambda i, at: (at[0], 0, 0)), by_rows]
            + extra,
            out_specs=[by_rows, pl.BlockSpec((rows, channels), lambda i, at: (i, 0))]
            + [pl.BlockSpec(memory_space=pltpu.VMEM)] * len(sums),
            scratch_shapes=([pltpu.VMEM((channels, tracks), f32)] if last else [])
            + [pltpu.VMEM((rows + 16, channels), f32)],
        ),
        out_shape=[
            pltpu.HBM((count, tracks), bf16),
            pltpu.HBM((PARTS * rows, channels), bf16),
            *sums,
        ],
        input_output_aliases={} if first else {at_input: 0},
        cost_estimate=pl.CostEstimate(
            flops=2 * PARTS * rows * (conv_w.size + 3 * head_w.size),
            transcendentals=4 * PARTS * rows * tracks,
            bytes_accessed=16 << 20,
        ),
        compiler_params=pltpu.CompilerParams(vmem_limit_bytes=HEADV << 20),
        name="head_pass",
    )(at, *operands, keep, targets, *(carried or ()))


def body(
    trunk,
    norm_gain,
    w_query,
    w_kv,
    w_out,
    w_up,
    skip,
    conv_w,
    head_w,
    head_bias,
    targets,
    missing,
    group_ids,
    group_weight,
):
    f32, bf16 = jnp.float32, jnp.bfloat16
    row_count = trunk.shape[0]
    head_dim = w_kv.shape[1] // 2
    head_count = w_query.shape[1] // head_dim
    widened = trunk.astype(f32)
    meansq = jnp.mean(widened * widened, axis=1, keepdims=True)
    normed = (widened * lax.rsqrt(meansq + 1e-06) * norm_gain).astype(bf16)
    keyvals = jnp.dot(normed, w_kv, preferred_element_type=f32).astype(bf16)
    skip_parts = [moved(skip, 1, step) for step in (1, 2, 3)]
    for dim in (2, 1):
        keyvals = join(keyvals, *[moved(keyvals, dim, step) for step in (1, 3, 2)])
    skip_parts, keyvals = lax.optimization_barrier((skip_parts, keyvals))
    skip_run = join(skip, *skip_parts)
    queries = jnp.dot(normed, w_query, preferred_element_type=f32).astype(bf16)
    crossed = moved(keyvals, 3, 1)
    pieces = [moved(keyvals, 0, step) for step in (1, 3, 2)]
    skips = [skip_run, moved(skip_run, 2, 2)]
    state = attend(None, queries, [keyvals], head_dim)
    for piece in pieces:
        state = attend(state, queries, [crossed, piece], head_dim)
        crossed = moved(piece, 3, 1)
    state = attend(state, queries, [crossed], head_dim)
    state, skips = lax.optimization_barrier((state, skips))
    upward = project(state, trunk, w_out, w_up)
    up_pair = join(upward, moved(upward, 2, 2))
    ups = [up_pair] + [moved(up_pair, 1, step) for step in (1, 2, 3)]
    y, zh, core = lax.axis_index("y"), lax.axis_index("zh"), lax.axis_index("core")
    wide, edge_first, edge_last = expand(jnp.stack([y, zh]).astype(jnp.int32), ups, skips)
    tap_count, channels = conv_w.shape[:2]
    rim = tap_count // 2
    pos_count = targets.shape[0]
    n_bin = lax.axis_size(BIN)
    up_pairs = [(i, i + 1) for i in range(n_bin - 1)]
    before = lax.ppermute(edge_last, BIN, up_pairs)
    after = lax.ppermute(edge_first, BIN, [(j, i) for i, j in up_pairs])
    tile_width = head_w.shape[1]
    groups = group_weight.shape[0]
    total_tracks = group_ids.shape[0]
    labels = jnp.arange(groups, dtype=jnp.int32)
    counts = jnp.sum((group_ids == labels[None, :]).astype(jnp.int32), axis=0)
    per_group = group_weight * total_tracks / (groups * counts.astype(f32))
    local_ids = lax.dynamic_slice_in_dim(group_ids, lax.axis_index(TRK) * tile_width, tile_width, 0)
    track_scale = jnp.sum(jnp.where(local_ids == labels[None, :], per_group[None, :], 0.0), axis=1)
    keep_mask = 1.0 - missing.astype(f32).reshape(4, 1, missing.shape[0] // 4)
    targets = pltpu.with_memory_space_constraint(targets, pltpu.HBM)
    carried, received = None, []
    for step in (2, 1, 3, 0):
        if step == 0:
            before, received[0] = lax.optimization_barrier((before, received[0]))
        prediction, partial, *total = head_pass(
            jnp.stack([lax.rem(y + step, 4), core]).astype(jnp.int32),
            carried,
            wide,
            before,
            after,
            conv_w,
            head_w,
            head_bias[None, :],
            track_scale[None, :],
            keep_mask,
            targets,
            step == 0,
            pos_count * n_bin,
        )
        carried = (prediction, *total)
        received.append(moved(partial, 1, step) if step else partial)
    mine, theirs = total
    theirs, received[1] = lax.optimization_barrier((theirs, received[1]))
    summed = sum(part.astype(f32) for part in received)
    halves = summed.reshape(2, summed.shape[0] // 2, channels)
    away = lax.dynamic_index_in_dim(halves, 1 - zh, 0, keepdims=False).astype(bf16)
    here = lax.dynamic_index_in_dim(halves, zh, 0, keepdims=False)
    feature_grad = (here + moved(away, 2, 2).astype(f32)).astype(bf16)
    pair_sum = (mine + lax.ppermute(theirs, "core", [(0, 1), (1, 0)]).astype(f32)).astype(bf16)
    pair_sum = pair_sum.reshape(lax.axis_size("bz"), channels // n_bin, tile_width)
    gathered = lax.all_to_all(pair_sum, "bz", 0, 0, tiled=True)
    head_grad = jnp.sum(gathered.astype(f32), axis=0)
    return (prediction, head_grad, feature_grad)


def solution(mesh):
    inner = Mesh(np.asarray(mesh.devices).reshape(8, 2, 4, 2), ALL)
    in_specs = (
        P(ALL, None),
        P(),
        P(),
        P(),
        P(),
        P(),
        P(ALL, None),
        P(),
        P(None, TRK),
        P(TRK),
        P(BIN, TRK),
        P(BIN),
        P(),
        P(),
    )
    out_specs = (P(BIN, TRK), P(BIN, TRK), P(ALL, None))
    return jax.shard_map(body, mesh=inner, in_specs=in_specs, out_specs=out_specs, check_vma=False)
```

```python
import functools
import math

import jax
import jax.numpy as jnp
import numpy as np
from jax import lax
from jax.experimental import pallas as pl
from jax.experimental.pallas import tpu as pltpu
from jax.sharding import Mesh, PartitionSpec as P

logit_cap = 20.0
BIN = ("bz", "core")
TRK = ("y", "zh")
ALL = BIN + TRK


def place(index):
    bz, rest = divmod(index, 16)
    core, rest = divmod(rest, 8)
    y, zh = divmod(rest, 2)
    zlo, x = divmod(bz, 4)
    return (x, y, zh * 2 + zlo, core)


def number(x, y, z, core):
    zh, zlo = divmod(z, 2)
    return ((zlo * 4 + x) * 2 + core) * 8 + y * 2 + zh


def moved(value, dim, step):
    sizes = (4, 4, 4, 2)
    pairs = []
    for index in range(128):
        target = list(place(index))
        target[dim] = (target[dim] + step) % sizes[dim]
        pairs.append((index, number(*target)))
    return lax.ppermute(value, ALL, pairs)


def whole(array):
    return pl.BlockSpec(array.shape, lambda *_: (0,) * array.ndim, pipeline_mode=pl.Buffered(1))


def join_kernel(*refs):
    out = refs[-1]
    rows = refs[0].shape[0]
    for index, ref in enumerate(refs[:-1]):
        out[index * rows : (index + 1) * rows, :] = ref[...]


def join(*pieces):
    rows, columns = pieces[0].shape
    out = jax.ShapeDtypeStruct((len(pieces) * rows, columns), pieces[0].dtype)
    return pl.pallas_call(
        join_kernel,
        in_specs=[pl.BlockSpec(memory_space=pltpu.VMEM)] * len(pieces),
        out_specs=pl.BlockSpec(memory_space=pltpu.VMEM),
        out_shape=out,
        cost_estimate=pl.CostEstimate(flops=0, transcendentals=0, bytes_accessed=4 * out.size),
        compiler_params=pltpu.CompilerParams(vmem_limit_bytes=4 << 20),
        name="join",
    )(*pieces)


def attend_kernel(head_dim, first, *refs):
    q_ref, refs = refs[0], refs[1:]
    num_ref, den_ref = refs[-2:]
    pieces = refs[:-2] if first else refs[:-4]
    f32, bf16 = jnp.float32, jnp.bfloat16
    heads = q_ref.shape[1] // head_dim
    queries = jnp.concatenate(
        [q_ref[:, h * head_dim : (h + 1) * head_dim] for h in range(heads)], 0
    )
    inner = 1.0 / (math.sqrt(head_dim) * logit_cap)
    outer = logit_cap * math.log2(math.e)
    num = jnp.zeros(num_ref.shape, f32) if first else refs[-4][...]
    den = jnp.zeros(den_ref.shape, f32) if first else refs[-3][...]
    step = 256
    for piece in pieces:
        for start in range(0, piece.shape[0], step):
            keys = piece[start : start + step, :head_dim]
            values = piece[start : start + step, head_dim:]
            scores = lax.dot_general(
                queries, keys, (((1,), (1,)), ((), ())), preferred_element_type=f32
            )
            weights = jnp.exp2(outer * jnp.tanh(scores * inner))
            num = num + jnp.dot(weights.astype(bf16), values, preferred_element_type=f32)
            for lane in range(0, step, 128):
                den = den + weights[:, lane : lane + 128]
    num_ref[...] = num
    den_ref[...] = den


def attend(state, queries, pieces, head_dim):
    rows = queries.shape[0] * queries.shape[1] // head_dim
    operands = [queries, *pieces, *(state or ())]
    keys = sum(piece.shape[0] for piece in pieces)
    return pl.pallas_call(
        functools.partial(attend_kernel, head_dim, state is None),
        grid=(1,),
        in_specs=[whole(operand) for operand in operands],
        out_specs=[pl.BlockSpec((rows, head_dim), lambda i: (0, 0))] * 2,
        out_shape=[jax.ShapeDtypeStruct((rows, head_dim), jnp.float32)] * 2,
        cost_estimate=pl.CostEstimate(
            flops=8 * rows * keys * head_dim,
            transcendentals=2 * rows * keys,
            bytes_accessed=1 << 20,
        ),
        compiler_params=pltpu.CompilerParams(vmem_limit_bytes=8 << 20),
        name="attend",
    )(*operands)


def project_kernel(num_ref, den_ref, trunk_ref, out_ref, up_ref, skip_ref, wide_ref, first_ref, last_ref):
    f32, bf16 = jnp.float32, jnp.bfloat16
    rows, positions = trunk_ref.shape[0], skip_ref.shape[0]
    total = jnp.sum(den_ref[...], axis=1, keepdims=True)
    ratio = (num_ref[...] / total).astype(bf16)
    heads = ratio.shape[0] // rows
    attended = jnp.concatenate([ratio[h * rows : (h + 1) * rows] for h in range(heads)], 1)
    hidden = (
        trunk_ref[...].astype(f32)
        + jnp.dot(attended, out_ref[...], preferred_element_type=f32)
    ).astype(bf16)
    upward = jnp.dot(hidden, up_ref[...], preferred_element_type=f32)
    factor = positions // rows
    for row in range(rows):
        part = slice(row * factor, (row + 1) * factor)
        wide_ref[part, :] = jnp.broadcast_to(upward[row : row + 1, :], (factor, upward.shape[1]))
    upsampled = (wide_ref[...] + skip_ref[...].astype(f32)).astype(bf16)
    wide_ref[...] = upsampled.astype(f32)
    first_ref[...] = wide_ref[0:8, :].astype(bf16)
    last_ref[...] = wide_ref[positions - 8 : positions, :].astype(bf16)


def project(state, trunk, w_out, w_up, skip):
    operands = (*state, trunk, w_out, w_up, skip)
    edge = jax.ShapeDtypeStruct((8, skip.shape[1]), jnp.bfloat16)
    return pl.pallas_call(
        project_kernel,
        in_specs=[pl.BlockSpec(memory_space=pltpu.VMEM)] * len(operands),
        out_specs=[pl.BlockSpec(memory_space=pltpu.VMEM)] * 3,
        out_shape=[jax.ShapeDtypeStruct(skip.shape, jnp.float32), edge, edge],
        cost_estimate=pl.CostEstimate(
            flops=2 * trunk.shape[0] * (w_out.size + w_up.size),
            transcendentals=0,
            bytes_accessed=2 * (w_out.size + w_up.size),
        ),
        compiler_params=pltpu.CompilerParams(vmem_limit_bytes=8 << 20),
        name="project",
    )(*operands)


def conv_kernel(wide_ref, before_ref, after_ref, conv_ref, feature_ref, near):
    f32, bf16 = jnp.float32, jnp.bfloat16
    rows, channels = wide_ref.shape
    taps = conv_ref.shape[0]
    rim = taps // 2
    near[0:8, :] = before_ref[...].astype(f32)
    near[8 : rows + 8, :] = wide_ref[...]
    near[rows + 8 : rows + 16, :] = after_ref[...].astype(f32)
    conved = jnp.zeros((rows, channels), f32)
    for tap in range(taps):
        begin = 8 - rim + tap
        conved = conved + jnp.dot(
            near[begin : begin + rows, :].astype(bf16), conv_ref[tap], preferred_element_type=f32
        )
    cubic = math.sqrt(2.0 / math.pi) * (conved + 0.044715 * (conved * conved * conved))
    feature_ref[...] = (wide_ref[...] + 0.5 * conved * (1.0 + jnp.tanh(cubic))).astype(bf16)


def convolve(wide, before, after, conv_w):
    operands = (wide, before, after, conv_w)
    return pl.pallas_call(
        conv_kernel,
        in_specs=[pl.BlockSpec(memory_space=pltpu.VMEM)] * len(operands),
        out_specs=pl.BlockSpec(memory_space=pltpu.VMEM),
        out_shape=jax.ShapeDtypeStruct(wide.shape, jnp.bfloat16),
        scratch_shapes=[pltpu.VMEM((wide.shape[0] + 16, wide.shape[1]), jnp.float32)],
        cost_estimate=pl.CostEstimate(
            flops=2 * wide.shape[0] * conv_w.size,
            transcendentals=wide.size,
            bytes_accessed=2 * conv_w.size,
        ),
        compiler_params=pltpu.CompilerParams(vmem_limit_bytes=10 << 20),
        name="convolve",
    )(*operands)


def head_kernel(
    first, last, positions, at_ref, near_ref, far_ref, head_ref, bias_ref, scale_ref, keep_ref, target_ref,
    *refs,
):
    f32, bf16 = jnp.float32, jnp.bfloat16
    if not first:
        old_ref, refs = refs[1], refs[2:]
    pred_ref, partial_ref, sums = refs[0], refs[1], refs[2:]
    total_ref = sums[-1]
    step = pl.program_id(0)
    rows, channels = partial_ref.shape
    bins = keep_ref.shape[2]
    factor = rows // bins
    row = lax.broadcasted_iota(jnp.int32, (rows, bins), 0)
    col = lax.broadcasted_iota(jnp.int32, (rows, bins), 1) * factor
    spread = jnp.where((row >= col) & (row < col + factor), 1.0, 0.0).astype(bf16)
    keep = lax.dot_general(
        spread,
        jnp.broadcast_to(keep_ref[0].astype(bf16), (8, bins)),
        (((1,), (1,)), ((), ())),
        preferred_element_type=f32,
    )[:, :1]
    feature = jnp.where(step == 0, near_ref[...], far_ref[...])
    logits = jnp.dot(feature, head_ref[...], preferred_element_type=f32) + bias_ref[...]
    decay = jnp.exp(-jnp.abs(logits))
    smooth = jnp.maximum(logits, 0.0) + jnp.log1p(decay)
    sigmoid = jnp.where(logits >= 0.0, 1.0, decay) / (1.0 + decay)
    pred_ref[...] = smooth.astype(bf16)
    misfit = smooth - target_ref[...].astype(f32)
    slope = (keep * scale_ref[...] * misfit * sigmoid).astype(bf16)
    partial_ref[...] = lax.dot_general(
        slope, head_ref[...], (((1,), (1,)), ((), ())), preferred_element_type=f32
    ).astype(bf16)
    product = lax.dot_general(
        feature, slope, (((0,), (0,)), ((), ())), preferred_element_type=f32
    )

    @pl.when(step == 0)
    def _():
        total_ref[...] = product if first else product + old_ref[...]

    @pl.when(step > 0)
    def _():
        total_ref[...] += product

    @pl.when(step == 1)
    def _():
        if not last:
            return
        mine_ref, theirs_ref = sums[:2]
        core, height = at_ref[0], channels // 16
        for pair in range(8):
            at = pl.multiple_of((2 * pair + core) * height, height)
            other = pl.multiple_of((2 * pair + 1 - core) * height, height)
            into = slice(pair * height, (pair + 1) * height)
            mine_ref[into, :] = total_ref[pl.ds(at, height), :] / positions
            theirs_ref[into, :] = (total_ref[pl.ds(other, height), :] / positions).astype(bf16)


def head_pass(at, carried, feature, head_w, bias, scale, keep, targets, last, positions):
    f32, bf16 = jnp.float32, jnp.bfloat16
    count, tracks = targets.shape
    channels = head_w.shape[0]
    rows = count // 8
    first = carried is None

    def segment(i, at):
        return at[1] * 2 + jnp.abs(at[2] - i)

    by_rows = pl.BlockSpec((rows, tracks), lambda i, at: (segment(i, at), 0))
    by_step = pl.BlockSpec((rows, channels), lambda i, at: (i, 0))
    vmem = pl.BlockSpec(memory_space=pltpu.VMEM)
    totals = jax.ShapeDtypeStruct((channels, tracks), f32)
    half = (channels // 2, tracks)
    sums = [jax.ShapeDtypeStruct(half, f32), jax.ShapeDtypeStruct(half, bf16)] if last else [totals]
    return pl.pallas_call(
        functools.partial(head_kernel, first, last, positions),
        grid_spec=pltpu.PrefetchScalarGridSpec(
            num_scalar_prefetch=1,
            grid=(2,),
            in_specs=[vmem] * 5
            + [pl.BlockSpec((1,) + keep.shape[1:], lambda i, at: (segment(i, at), 0, 0)), by_rows]
            + ([] if first else [pl.BlockSpec(memory_space=pl.ANY), vmem]),
            out_specs=[by_rows, by_step] + [vmem] * len(sums),
            scratch_shapes=[pltpu.VMEM((channels, tracks), f32)] if last else [],
        ),
        out_shape=[
            pltpu.HBM((count, tracks), bf16),
            jax.ShapeDtypeStruct((2 * rows, channels), bf16),
            *sums,
        ],
        input_output_aliases={} if first else {8: 0},
        cost_estimate=pl.CostEstimate(
            flops=12 * rows * head_w.size,
            transcendentals=8 * rows * tracks,
            bytes_accessed=6 << 20,
        ),
        compiler_params=pltpu.CompilerParams(vmem_limit_bytes=16 << 20),
        name="head_pass",
    )(at, *feature, head_w, bias, scale, keep, targets, *(carried or ()))


def body(
    trunk,
    norm_gain,
    w_query,
    w_kv,
    w_out,
    w_up,
    skip,
    conv_w,
    head_w,
    head_bias,
    targets,
    missing,
    group_ids,
    group_weight,
):
    f32, bf16 = jnp.float32, jnp.bfloat16
    row_count = trunk.shape[0]
    head_dim = w_kv.shape[1] // 2
    head_count = w_query.shape[1] // head_dim
    widened = trunk.astype(f32)
    meansq = jnp.mean(widened * widened, axis=1, keepdims=True)
    normed = (widened * lax.rsqrt(meansq + 1e-06) * norm_gain).astype(bf16)
    keyvals = jnp.dot(normed, w_kv, preferred_element_type=f32).astype(bf16)
    for dim in (2, 1):
        keyvals = join(keyvals, *[moved(keyvals, dim, step) for step in (1, 3, 2)])
    queries = jnp.dot(normed, w_query, preferred_element_type=f32).astype(bf16)
    crossed = moved(keyvals, 3, 1)
    pieces = [moved(keyvals, 0, step) for step in (1, 3, 2)]
    state = attend(None, queries, [keyvals], head_dim)
    for piece in pieces:
        state = attend(state, queries, [crossed, piece], head_dim)
        crossed = moved(piece, 3, 1)
    state = attend(state, queries, [crossed], head_dim)
    wide, edge_first, edge_last = project(state, trunk, w_out, w_up, skip)
    channels = conv_w.shape[1]
    pos_count = targets.shape[0]
    n_bin, n_all = lax.axis_size(BIN), lax.axis_size(ALL)
    ups = [(i, i + 1) for i in range(n_all - 1)]
    before = lax.ppermute(edge_last, ALL, ups)
    after = lax.ppermute(edge_first, ALL, [(j, i) for i, j in ups])
    feature = convolve(wide, before, after, conv_w)
    features = {0: (feature, moved(feature, 2, 2))}
    for step in (2, 1, 3):
        near = moved(feature, 1, step)
        features[step] = (near, moved(near, 2, 2))
    y, zh, core = lax.axis_index("y"), lax.axis_index("zh"), lax.axis_index("core")
    tile_width = head_w.shape[1]
    groups = group_weight.shape[0]
    total_tracks = group_ids.shape[0]
    labels = jnp.arange(groups, dtype=jnp.int32)
    counts = jnp.sum((group_ids == labels[None, :]).astype(jnp.int32), axis=0)
    per_group = group_weight * total_tracks / (groups * counts.astype(f32))
    local_ids = lax.dynamic_slice_in_dim(group_ids, lax.axis_index(TRK) * tile_width, tile_width, 0)
    track_scale = jnp.sum(jnp.where(local_ids == labels[None, :], per_group[None, :], 0.0), axis=1)
    keep_mask = 1.0 - missing.astype(f32).reshape(8, 1, missing.shape[0] // 8)
    targets = pltpu.with_memory_space_constraint(targets, pltpu.HBM)
    carried, received = None, []
    for step in (2, 1, 3, 0):
        if step == 0:
            features[0], received[0] = lax.optimization_barrier((features[0], received[0]))
        prediction, partial, *total = head_pass(
            jnp.stack([core, lax.rem(y + 4 - step, 4), zh]).astype(jnp.int32),
            carried,
            features[step],
            head_w,
            head_bias[None, :],
            track_scale[None, :],
            keep_mask,
            targets,
            step == 0,
            pos_count * n_bin,
        )
        carried = (prediction, *total)
        received.append(moved(partial, 1, 4 - step) if step else partial)
    mine, theirs = total
    theirs, received[1] = lax.optimization_barrier((theirs, received[1]))
    summed = sum(part.astype(f32) for part in received)
    half = summed.shape[0] // 2
    away = summed[half:].astype(bf16)
    feature_grad = (summed[:half] + moved(away, 2, 2).astype(f32)).astype(bf16)
    pair_sum = (mine + lax.ppermute(theirs, "core", [(0, 1), (1, 0)]).astype(f32)).astype(bf16)
    pair_sum = pair_sum.reshape(lax.axis_size("bz"), channels // n_bin, tile_width)
    gathered = lax.all_to_all(pair_sum, "bz", 0, 0, tiled=True)
    head_grad = jnp.sum(gathered.astype(f32), axis=0)
    return (prediction, head_grad, feature_grad)


def solution(mesh):
    inner = Mesh(np.asarray(mesh.devices).reshape(8, 2, 4, 2), ALL)
    in_specs = (
        P(ALL, None),
        P(),
        P(),
        P(),
        P(),
        P(),
        P(ALL, None),
        P(),
        P(None, TRK),
        P(TRK),
        P(BIN, TRK),
        P(BIN),
        P(),
        P(),
    )
    out_specs = (P(BIN, TRK), P(BIN, TRK), P(ALL, None))
    return jax.shard_map(body, mesh=inner, in_specs=in_specs, out_specs=out_specs, check_vma=False)
```

```python
import functools
import math

import jax
import jax.numpy as jnp
import numpy as np
from jax import lax
from jax.experimental import pallas as pl
from jax.experimental.pallas import tpu as pltpu
from jax.sharding import Mesh, PartitionSpec as P

logit_cap = 20.0
ORDER = ((2,), (1,), (3,), (0,))
BIN = ("bz", "core")
TRK = ("y", "zh")
ALL = BIN + TRK


def place(index):
    bz, rest = divmod(index, 16)
    core, rest = divmod(rest, 8)
    y, zh = divmod(rest, 2)
    zlo, x = divmod(bz, 4)
    return (x, y, zh * 2 + zlo, core)


def number(x, y, z, core):
    zh, zlo = divmod(z, 2)
    return ((zlo * 4 + x) * 2 + core) * 8 + y * 2 + zh


def moved(value, dim, step):
    sizes = (4, 4, 4, 2)
    pairs = []
    for index in range(128):
        target = list(place(index))
        target[dim] = (target[dim] + step) % sizes[dim]
        pairs.append((index, number(*target)))
    return lax.ppermute(value, ALL, pairs)


def whole(array):
    return pl.BlockSpec(array.shape, lambda *_: (0,) * array.ndim, pipeline_mode=pl.Buffered(1))


def join_kernel(*refs):
    out = refs[-1]
    rows = refs[0].shape[0]
    for index, ref in enumerate(refs[:-1]):
        out[index * rows : (index + 1) * rows, :] = ref[...]


def join(*pieces):
    rows, columns = pieces[0].shape
    out = jax.ShapeDtypeStruct((len(pieces) * rows, columns), pieces[0].dtype)
    return pl.pallas_call(
        join_kernel,
        in_specs=[pl.BlockSpec(memory_space=pltpu.VMEM)] * len(pieces),
        out_specs=pl.BlockSpec(memory_space=pltpu.VMEM),
        out_shape=out,
        cost_estimate=pl.CostEstimate(flops=0, transcendentals=0, bytes_accessed=4 * out.size),
        compiler_params=pltpu.CompilerParams(vmem_limit_bytes=4 << 20),
        name="join",
    )(*pieces)


def normalized(value, gain):
    widened = value.astype(jnp.float32)
    meansq = jnp.mean(widened * widened, axis=1, keepdims=True)
    return (widened * lax.rsqrt(meansq + 1e-06) * gain).astype(jnp.bfloat16)


def start_kernel(trunk_ref, gain_ref, kv_ref, skip_ref, keyvals_ref, next_ref, prev_ref, tall):
    f32, bf16 = jnp.float32, jnp.bfloat16
    normed = normalized(trunk_ref[...], gain_ref[...])
    keyvals_ref[...] = jnp.dot(normed, kv_ref[...], preferred_element_type=f32).astype(bf16)
    rows, width = trunk_ref.shape
    positions, channels = skip_ref.shape
    count = width // channels
    widened = trunk_ref[...].astype(f32)
    for out, row, near in ((next_ref, rows - 1, positions - 8), (prev_ref, 0, 0)):
        tall[...] = skip_ref[near : near + 8, :].astype(f32)
        rim = tall[6:8, :] if row else tall[0:2, :]
        tall[count : count + 2, :] = rim
        for piece in range(count):
            tall[piece : piece + 1, :] = widened[
                row : row + 1, piece * channels : (piece + 1) * channels
            ]
        out[...] = tall[...].astype(bf16)


def start(trunk, gain, w_kv, skip):
    vmem = pl.BlockSpec(memory_space=pltpu.VMEM)
    edge = jax.ShapeDtypeStruct((8, skip.shape[1]), jnp.bfloat16)
    return pl.pallas_call(
        start_kernel,
        grid=(1,),
        in_specs=[whole(operand) for operand in (trunk, gain, w_kv, skip)],
        out_specs=[vmem] * 3,
        out_shape=[jax.ShapeDtypeStruct((trunk.shape[0], w_kv.shape[1]), jnp.bfloat16), edge, edge],
        scratch_shapes=[pltpu.VMEM(edge.shape, jnp.float32)],
        cost_estimate=pl.CostEstimate(
            flops=2 * trunk.shape[0] * w_kv.size, transcendentals=64, bytes_accessed=2 * w_kv.size
        ),
        compiler_params=pltpu.CompilerParams(vmem_limit_bytes=6 << 20),
        name="start",
    )(trunk, gain, w_kv, skip)


def query_kernel(trunk_ref, gain_ref, before_ref, after_ref, w_ref, queries_ref, rims_ref, tall):
    f32, bf16 = jnp.float32, jnp.bfloat16
    rows, width = trunk_ref.shape
    channels, head_dim = before_ref.shape[1], rims_ref.shape[1]
    sides = [
        jnp.concatenate(
            [ref[piece : piece + 1, :].astype(f32) for piece in range(width // channels)], 1
        )
        for ref in (before_ref, after_ref)
    ]
    every = jnp.concatenate(
        [trunk_ref[...].astype(f32)] + sides + [jnp.zeros((14, width), f32)], 0
    )
    normed = normalized(every, gain_ref[...])
    projected = jnp.dot(normed, w_ref[...], preferred_element_type=f32)
    queries_ref[...] = projected[:rows].astype(bf16)
    for head in range(projected.shape[1] // head_dim):
        tall[2 * head : 2 * head + 2, :] = projected[
            rows : rows + 2, head * head_dim : (head + 1) * head_dim
        ]
    rims_ref[...] = tall[...].astype(bf16)


def query(trunk, gain, before, after, w_query, head_dim):
    vmem = pl.BlockSpec(memory_space=pltpu.VMEM)
    rims = (2 * w_query.shape[1] // head_dim, head_dim)
    return pl.pallas_call(
        query_kernel,
        in_specs=[vmem] * 5,
        out_specs=[vmem] * 2,
        out_shape=[
            jax.ShapeDtypeStruct((trunk.shape[0], w_query.shape[1]), jnp.bfloat16),
            jax.ShapeDtypeStruct(rims, jnp.bfloat16),
        ],
        scratch_shapes=[pltpu.VMEM(rims, jnp.float32)],
        cost_estimate=pl.CostEstimate(
            flops=2 * trunk.shape[0] * w_query.size,
            transcendentals=64,
            bytes_accessed=2 * w_query.size,
        ),
        compiler_params=pltpu.CompilerParams(vmem_limit_bytes=8 << 20),
        name="query",
    )(trunk, gain, before, after, w_query)


def attend_kernel(head_dim, first, *refs):
    q_ref, rim_ref, refs = refs[0], refs[1], refs[2:]
    num_ref, den_ref = refs[-2:]
    pieces = refs[:-2] if first else refs[:-4]
    f32, bf16 = jnp.float32, jnp.bfloat16
    heads = q_ref.shape[1] // head_dim
    queries = jnp.concatenate(
        [q_ref[:, h * head_dim : (h + 1) * head_dim] for h in range(heads)] + [rim_ref[...]], 0
    )
    inner = 1.0 / (math.sqrt(head_dim) * logit_cap)
    outer = logit_cap * math.log2(math.e)
    num = jnp.zeros(num_ref.shape, f32) if first else refs[-4][...]
    den = jnp.zeros(den_ref.shape, f32) if first else refs[-3][...]
    step = 256
    for piece in pieces:
        for start in range(0, piece.shape[0], step):
            keys = piece[start : start + step, :head_dim]
            values = piece[start : start + step, head_dim:]
            scores = lax.dot_general(
                queries, keys, (((1,), (1,)), ((), ())), preferred_element_type=f32
            )
            weights = jnp.exp2(outer * jnp.tanh(scores * inner))
            num = num + jnp.dot(weights.astype(bf16), values, preferred_element_type=f32)
            for lane in range(0, step, 128):
                den = den + weights[:, lane : lane + 128]
    num_ref[...] = num
    den_ref[...] = den


def attend(state, queries, pieces, head_dim):
    rows = queries[0].size // head_dim + queries[1].shape[0]
    operands = [*queries, *pieces, *(state or ())]
    keys = sum(piece.shape[0] for piece in pieces)
    return pl.pallas_call(
        functools.partial(attend_kernel, head_dim, state is None),
        grid=(1,),
        in_specs=[whole(operand) for operand in operands],
        out_specs=[pl.BlockSpec((rows, head_dim), lambda i: (0, 0))] * 2,
        out_shape=[jax.ShapeDtypeStruct((rows, head_dim), jnp.float32)] * 2,
        cost_estimate=pl.CostEstimate(
            flops=8 * rows * keys * head_dim,
            transcendentals=2 * rows * keys,
            bytes_accessed=1 << 20,
        ),
        compiler_params=pltpu.CompilerParams(vmem_limit_bytes=8 << 20),
        name="attend",
    )(*operands)


def finish_kernel(
    at_ref, num_ref, den_ref, trunk_ref, before_ref, after_ref, out_ref, up_ref, skip_ref, conv_ref,
    feature_ref, ratio, near,
):
    f32, bf16 = jnp.float32, jnp.bfloat16
    rows, positions = trunk_ref.shape[0], skip_ref.shape[0]
    width, channels = trunk_ref.shape[1], skip_ref.shape[1]
    taps = conv_ref.shape[0]
    rim = taps // 2
    ratio[...] = num_ref[...] / jnp.sum(den_ref[...], axis=1, keepdims=True)
    heads = (ratio.shape[0] - 16) // rows
    attended = jnp.concatenate([ratio[h * rows : (h + 1) * rows, :] for h in range(heads)], 1)
    edge = jnp.concatenate(
        [ratio[heads * rows + 2 * h : heads * rows + 2 * h + 2, :] for h in range(heads)], 1
    )
    edge = jnp.concatenate([edge, jnp.zeros((14, edge.shape[1]), f32)], 0)
    attended = jnp.concatenate([attended.astype(bf16), edge.astype(bf16)], 0)
    sides = [
        jnp.concatenate(
            [ref[piece : piece + 1, :] for piece in range(width // channels)], 1
        ).astype(f32)
        for ref in (before_ref, after_ref)
    ]
    residual = jnp.concatenate(
        [trunk_ref[...].astype(f32)] + sides + [jnp.zeros((14, width), f32)], 0
    )
    hidden = (residual + jnp.dot(attended, out_ref[...], preferred_element_type=f32)).astype(bf16)
    upward = jnp.dot(hidden, up_ref[...], preferred_element_type=f32)
    factor = positions // rows
    for row in range(rows):
        begin = 8 + row * factor
        near[begin : begin + factor, :] = jnp.broadcast_to(
            upward[row : row + 1, :], (factor, channels)
        )
    inside = near[8 : 8 + positions, :] + skip_ref[...].astype(f32)
    near[8 : 8 + positions, :] = inside.astype(bf16).astype(f32)
    for index, (ref, begin) in enumerate(((before_ref, 8 - rim), (after_ref, 8 + positions))):
        tall = upward[rows + index : rows + index + 1, :] + ref[rim : 2 * rim, :].astype(f32)
        tall = tall.astype(bf16).astype(f32)
        near[begin : begin + rim, :] = jnp.where(at_ref[index] > 0, tall, 0.0)
    conved = jnp.zeros((positions, channels), f32)
    for tap in range(taps):
        begin = 8 - rim + tap
        conved = conved + jnp.dot(
            near[begin : begin + positions, :].astype(bf16),
            conv_ref[tap],
            preferred_element_type=f32,
        )
    cubic = math.sqrt(2.0 / math.pi) * (conved + 0.044715 * (conved * conved * conved))
    center = near[8 : 8 + positions, :]
    feature_ref[...] = (center + 0.5 * conved * (1.0 + jnp.tanh(cubic))).astype(bf16)


def finish(at, state, trunk, before, after, w_out, w_up, skip, conv_w):
    operands = (*state, trunk, before, after, w_out, w_up, skip, conv_w)
    vmem = pl.BlockSpec(memory_space=pltpu.VMEM)
    return pl.pallas_call(
        finish_kernel,
        in_specs=[pl.BlockSpec(memory_space=pltpu.SMEM)] + [vmem] * len(operands),
        out_specs=vmem,
        out_shape=jax.ShapeDtypeStruct(skip.shape, jnp.bfloat16),
        scratch_shapes=[
            pltpu.VMEM(state[0].shape, jnp.float32),
            pltpu.VMEM((skip.shape[0] + 16, skip.shape[1]), jnp.float32),
        ],
        cost_estimate=pl.CostEstimate(
            flops=2 * trunk.shape[0] * (w_out.size + w_up.size) + 2 * skip.shape[0] * conv_w.size,
            transcendentals=skip.size,
            bytes_accessed=2 * (w_out.size + w_up.size + conv_w.size),
        ),
        compiler_params=pltpu.CompilerParams(vmem_limit_bytes=14 << 20),
        name="finish",
    )(at, *operands)


def head_kernel(
    groups, first, last, positions, at_ref, *refs,
):
    f32, bf16 = jnp.float32, jnp.bfloat16
    halves, refs = refs[: 2 * groups], refs[2 * groups :]
    head_ref, bias_ref, scale_ref, keep_ref, target_ref = refs[:5]
    refs = refs[5:]
    if not first:
        old_ref, refs = refs[1], refs[2:]
    pred_ref, partials, sums = refs[0], refs[1 : 1 + groups], refs[1 + groups :]
    total_ref = sums[-1]
    step = pl.program_id(0)
    rows, channels = partials[0].shape
    bins = keep_ref.shape[2]
    factor = rows // bins
    row = lax.broadcasted_iota(jnp.int32, (rows, bins), 0)
    col = lax.broadcasted_iota(jnp.int32, (rows, bins), 1) * factor
    spread = jnp.where((row >= col) & (row < col + factor), 1.0, 0.0).astype(bf16)
    keep = lax.dot_general(
        spread,
        jnp.broadcast_to(keep_ref[0].astype(bf16), (8, bins)),
        (((1,), (1,)), ((), ())),
        preferred_element_type=f32,
    )[:, :1]
    feature = halves[-1][...]
    for index in range(len(halves) - 1):
        feature = jnp.where(step == index, halves[index][...], feature)
    logits = jnp.dot(feature, head_ref[...], preferred_element_type=f32) + bias_ref[...]
    decay = jnp.exp(-jnp.abs(logits))
    smooth = jnp.maximum(logits, 0.0) + jnp.log1p(decay)
    sigmoid = jnp.where(logits >= 0.0, 1.0, decay) / (1.0 + decay)
    pred_ref[...] = smooth.astype(bf16)
    misfit = smooth - target_ref[...].astype(f32)
    slope = (keep * scale_ref[...] * misfit * sigmoid).astype(bf16)
    partial = lax.dot_general(
        slope, head_ref[...], (((1,), (1,)), ((), ())), preferred_element_type=f32
    ).astype(bf16)
    for group in range(groups):

        @pl.when(lax.div(step, 2) == group)
        def _(group=group):
            partials[group][...] = partial

    product = lax.dot_general(
        feature, slope, (((0,), (0,)), ((), ())), preferred_element_type=f32
    )

    @pl.when(step == 0)
    def _():
        total_ref[...] = product if first else product + old_ref[...]

    @pl.when(step > 0)
    def _():
        total_ref[...] += product

    @pl.when(step == 2 * groups - 1)
    def _():
        if not last:
            return
        mine_ref, theirs_ref = sums[:2]
        core, height = at_ref[0], channels // 16
        for pair in range(8):
            at = pl.multiple_of((2 * pair + core) * height, height)
            other = pl.multiple_of((2 * pair + 1 - core) * height, height)
            into = slice(pair * height, (pair + 1) * height)
            mine_ref[into, :] = total_ref[pl.ds(at, height), :] / positions
            theirs_ref[into, :] = (total_ref[pl.ds(other, height), :] / positions).astype(bf16)


def head_pass(groups, at, carried, feature, head_w, bias, scale, keep, targets, last, positions):
    f32, bf16 = jnp.float32, jnp.bfloat16
    count, tracks = targets.shape
    channels = head_w.shape[0]
    rows = count // 8
    first = carried is None

    def segment(i, at):
        return at[2 + i // 2] * 2 + jnp.abs(at[1] - i % 2)

    by_rows = pl.BlockSpec((rows, tracks), lambda i, at: (segment(i, at), 0))
    by_group = [
        pl.BlockSpec((rows, channels), lambda i, at, g=g: (jnp.clip(i - 2 * g, 0, 1), 0))
        for g in range(groups)
    ]
    vmem = pl.BlockSpec(memory_space=pltpu.VMEM)
    totals = jax.ShapeDtypeStruct((channels, tracks), f32)
    half = (channels // 2, tracks)
    sums = [jax.ShapeDtypeStruct(half, f32), jax.ShapeDtypeStruct(half, bf16)] if last else [totals]
    return pl.pallas_call(
        functools.partial(head_kernel, groups, first, last, positions),
        grid_spec=pltpu.PrefetchScalarGridSpec(
            num_scalar_prefetch=1,
            grid=(2 * groups,),
            in_specs=[vmem] * (2 * groups + 3)
            + [pl.BlockSpec((1,) + keep.shape[1:], lambda i, at: (segment(i, at), 0, 0)), by_rows]
            + ([] if first else [pl.BlockSpec(memory_space=pl.ANY), vmem]),
            out_specs=[by_rows] + by_group + [vmem] * len(sums),
            scratch_shapes=[pltpu.VMEM((channels, tracks), f32)] if last else [],
        ),
        out_shape=[
            pltpu.HBM((count, tracks), bf16),
            *[jax.ShapeDtypeStruct((2 * rows, channels), bf16)] * groups,
            *sums,
        ],
        input_output_aliases={} if first else {6 + 2 * groups: 0},
        cost_estimate=pl.CostEstimate(
            flops=12 * groups * rows * head_w.size,
            transcendentals=8 * groups * rows * tracks,
            bytes_accessed=6 << 20,
        ),
        compiler_params=pltpu.CompilerParams(vmem_limit_bytes=16 << 20),
        name="head_pass",
    )(at, *feature, head_w, bias, scale, keep, targets, *(carried or ()))


def body(
    trunk,
    norm_gain,
    w_query,
    w_kv,
    w_out,
    w_up,
    skip,
    conv_w,
    head_w,
    head_bias,
    targets,
    missing,
    group_ids,
    group_weight,
):
    f32, bf16 = jnp.float32, jnp.bfloat16
    row_count = trunk.shape[0]
    head_dim = w_kv.shape[1] // 2
    head_count = w_query.shape[1] // head_dim
    n_all, index = lax.axis_size(ALL), lax.axis_index(ALL)
    channels = conv_w.shape[1]
    gain = norm_gain[None, :]
    keyvals, to_next, to_prev = start(
        *[pltpu.with_memory_space_constraint(value, pltpu.HBM) for value in (trunk, gain, w_kv, skip)]
    )
    nexts = [(i, i + 1) for i in range(n_all - 1)]
    keyvals = join(keyvals, *[moved(keyvals, 2, step) for step in (1, 3, 2)])
    before = lax.ppermute(to_next, ALL, nexts)
    after = lax.ppermute(to_prev, ALL, [(j, i) for i, j in nexts])
    keyvals = join(keyvals, *[moved(keyvals, 1, step) for step in (1, 3, 2)])
    crossed = moved(keyvals, 3, 1)
    pieces = [moved(keyvals, 0, step) for step in (1, 3, 2)]
    pieces[0], before, after = lax.optimization_barrier((pieces[0], before, after))
    queries = query(trunk, gain, before, after, w_query, head_dim)
    pieces[1], queries = lax.optimization_barrier((pieces[1], queries))
    state = attend(None, queries, [keyvals], head_dim)
    for piece in pieces:
        state = attend(state, queries, [crossed, piece], head_dim)
        crossed = moved(piece, 3, 1)
    state = attend(state, queries, [crossed], head_dim)
    at = jnp.stack([index, n_all - 1 - index]).astype(jnp.int32)
    feature = finish(at, state, trunk, before, after, w_out, w_up, skip, conv_w)
    pos_count = targets.shape[0]
    n_bin = lax.axis_size(BIN)
    features = {0: (feature, moved(feature, 2, 2))}
    for step in (2, 1, 3):
        near = moved(feature, 1, step)
        features[step] = (near, moved(near, 2, 2))
    y, zh, core = lax.axis_index("y"), lax.axis_index("zh"), lax.axis_index("core")
    tile_width = head_w.shape[1]
    groups = group_weight.shape[0]
    total_tracks = group_ids.shape[0]
    labels = jnp.arange(groups, dtype=jnp.int32)
    counts = jnp.sum((group_ids == labels[None, :]).astype(jnp.int32), axis=0)
    per_group = group_weight * total_tracks / (groups * counts.astype(f32))
    local_ids = lax.dynamic_slice_in_dim(group_ids, lax.axis_index(TRK) * tile_width, tile_width, 0)
    track_scale = jnp.sum(jnp.where(local_ids == labels[None, :], per_group[None, :], 0.0), axis=1)
    keep_mask = 1.0 - missing.astype(f32).reshape(8, 1, missing.shape[0] // 8)
    targets = pltpu.with_memory_space_constraint(targets, pltpu.HBM)
    bias = head_bias[None, :]
    bias, far = lax.optimization_barrier((bias, features[0][1]))
    features[0] = (features[0][0], far)
    carried, received = None, {}
    for steps in ORDER:
        if 0 in steps:
            bias, received[2] = lax.optimization_barrier((bias, received[2]))
        prediction, *results = head_pass(
            len(steps),
            jnp.stack([core, zh] + [lax.rem(y + 4 - step, 4) for step in steps]).astype(jnp.int32),
            carried,
            [half for step in steps for half in features[step]],
            head_w,
            bias,
            track_scale[None, :],
            keep_mask,
            targets,
            0 in steps,
            pos_count * n_bin,
        )
        total = results[len(steps) :]
        carried = (prediction, *total)
        for step, partial in zip(steps, results):
            received[step] = moved(partial, 1, 4 - step) if step else partial
    mine, theirs = total
    theirs, received[1] = lax.optimization_barrier((theirs, received[1]))
    summed = sum(part.astype(f32) for part in received.values())
    half = summed.shape[0] // 2
    away = summed[half:].astype(bf16)
    feature_grad = (summed[:half] + moved(away, 2, 2).astype(f32)).astype(bf16)
    pair_sum = (mine + lax.ppermute(theirs, "core", [(0, 1), (1, 0)]).astype(f32)).astype(bf16)
    pair_sum = pair_sum.reshape(lax.axis_size("bz"), channels // n_bin, tile_width)
    gathered = lax.all_to_all(pair_sum, "bz", 0, 0, tiled=True)
    head_grad = jnp.sum(gathered.astype(f32), axis=0)
    return (prediction, head_grad, feature_grad)


def solution(mesh):
    inner = Mesh(np.asarray(mesh.devices).reshape(8, 2, 4, 2), ALL)
    in_specs = (
        P(ALL, None),
        P(),
        P(),
        P(),
        P(),
        P(),
        P(ALL, None),
        P(),
        P(None, TRK),
        P(TRK),
        P(BIN, TRK),
        P(BIN),
        P(),
        P(),
    )
    out_specs = (P(BIN, TRK), P(BIN, TRK), P(ALL, None))
    return jax.shard_map(body, mesh=inner, in_specs=in_specs, out_specs=out_specs, check_vma=False)
```

```python
import functools
import math

import jax
import jax.numpy as jnp
import numpy as np
from jax import lax
from jax.experimental import pallas as pl
from jax.experimental.pallas import tpu as pltpu
from jax.sharding import Mesh, PartitionSpec as P

logit_cap = 20.0
ORDER = ((2,), (1,), (3,), (0,))
BIN = ("bz", "core")
TRK = ("y", "zh")
ALL = BIN + TRK


def place(index):
    bz, rest = divmod(index, 16)
    core, rest = divmod(rest, 8)
    y, zh = divmod(rest, 2)
    zlo, x = divmod(bz, 4)
    return (x, y, zh * 2 + zlo, core)


def number(x, y, z, core):
    zh, zlo = divmod(z, 2)
    return ((zlo * 4 + x) * 2 + core) * 8 + y * 2 + zh


def moved(value, dim, step):
    sizes = (4, 4, 4, 2)
    pairs = []
    for index in range(128):
        target = list(place(index))
        target[dim] = (target[dim] + step) % sizes[dim]
        pairs.append((index, number(*target)))
    return lax.ppermute(value, ALL, pairs)


def whole(array):
    return pl.BlockSpec(array.shape, lambda *_: (0,) * array.ndim, pipeline_mode=pl.Buffered(1))


def join_kernel(*refs):
    out = refs[-1]
    rows = refs[0].shape[0]
    for index, ref in enumerate(refs[:-1]):
        out[index * rows : (index + 1) * rows, :] = ref[...]


def join(*pieces):
    rows, columns = pieces[0].shape
    out = jax.ShapeDtypeStruct((len(pieces) * rows, columns), pieces[0].dtype)
    return pl.pallas_call(
        join_kernel,
        in_specs=[pl.BlockSpec(memory_space=pltpu.VMEM)] * len(pieces),
        out_specs=pl.BlockSpec(memory_space=pltpu.VMEM),
        out_shape=out,
        cost_estimate=pl.CostEstimate(flops=0, transcendentals=0, bytes_accessed=4 * out.size),
        compiler_params=pltpu.CompilerParams(vmem_limit_bytes=4 << 20),
        name="join",
    )(*pieces)


def normalized(value, gain):
    widened = value.astype(jnp.float32)
    meansq = jnp.mean(widened * widened, axis=1, keepdims=True)
    return (widened * lax.rsqrt(meansq + 1e-06) * gain).astype(jnp.bfloat16)


def start_kernel(trunk_ref, gain_ref, kv_ref, skip_ref, keyvals_ref, next_ref, prev_ref, tall):
    f32, bf16 = jnp.float32, jnp.bfloat16
    normed = normalized(trunk_ref[...], gain_ref[...])
    keyvals_ref[...] = jnp.dot(normed, kv_ref[...], preferred_element_type=f32).astype(bf16)
    rows, width = trunk_ref.shape
    positions, channels = skip_ref.shape
    count = width // channels
    widened = trunk_ref[...].astype(f32)
    for out, row, near in ((next_ref, rows - 1, positions - 8), (prev_ref, 0, 0)):
        tall[...] = skip_ref[near : near + 8, :].astype(f32)
        rim = tall[6:8, :] if row else tall[0:2, :]
        tall[count : count + 2, :] = rim
        for piece in range(count):
            tall[piece : piece + 1, :] = widened[
                row : row + 1, piece * channels : (piece + 1) * channels
            ]
        out[...] = tall[...].astype(bf16)


def start(trunk, gain, w_kv, skip):
    vmem = pl.BlockSpec(memory_space=pltpu.VMEM)
    edge = jax.ShapeDtypeStruct((8, skip.shape[1]), jnp.bfloat16)
    return pl.pallas_call(
        start_kernel,
        grid=(1,),
        in_specs=[whole(operand) for operand in (trunk, gain, w_kv, skip)],
        out_specs=[vmem] * 3,
        out_shape=[jax.ShapeDtypeStruct((trunk.shape[0], w_kv.shape[1]), jnp.bfloat16), edge, edge],
        scratch_shapes=[pltpu.VMEM(edge.shape, jnp.float32)],
        cost_estimate=pl.CostEstimate(
            flops=2 * trunk.shape[0] * w_kv.size, transcendentals=64, bytes_accessed=2 * w_kv.size
        ),
        compiler_params=pltpu.CompilerParams(vmem_limit_bytes=6 << 20),
        name="start",
    )(trunk, gain, w_kv, skip)


def query_kernel(trunk_ref, gain_ref, before_ref, after_ref, w_ref, queries_ref, rims_ref, tall):
    f32, bf16 = jnp.float32, jnp.bfloat16
    rows, width = trunk_ref.shape
    channels, head_dim = before_ref.shape[1], rims_ref.shape[1]
    sides = [
        jnp.concatenate(
            [ref[piece : piece + 1, :].astype(f32) for piece in range(width // channels)], 1
        )
        for ref in (before_ref, after_ref)
    ]
    every = jnp.concatenate(
        [trunk_ref[...].astype(f32)] + sides + [jnp.zeros((14, width), f32)], 0
    )
    normed = normalized(every, gain_ref[...])
    projected = jnp.dot(normed, w_ref[...], preferred_element_type=f32)
    queries_ref[...] = projected[:rows].astype(bf16)
    for head in range(projected.shape[1] // head_dim):
        tall[2 * head : 2 * head + 2, :] = projected[
            rows : rows + 2, head * head_dim : (head + 1) * head_dim
        ]
    rims_ref[...] = tall[...].astype(bf16)


def query(trunk, gain, before, after, w_query, head_dim):
    vmem = pl.BlockSpec(memory_space=pltpu.VMEM)
    rims = (2 * w_query.shape[1] // head_dim, head_dim)
    return pl.pallas_call(
        query_kernel,
        in_specs=[vmem] * 5,
        out_specs=[vmem] * 2,
        out_shape=[
            jax.ShapeDtypeStruct((trunk.shape[0], w_query.shape[1]), jnp.bfloat16),
            jax.ShapeDtypeStruct(rims, jnp.bfloat16),
        ],
        scratch_shapes=[pltpu.VMEM(rims, jnp.float32)],
        cost_estimate=pl.CostEstimate(
            flops=2 * trunk.shape[0] * w_query.size,
            transcendentals=64,
            bytes_accessed=2 * w_query.size,
        ),
        compiler_params=pltpu.CompilerParams(vmem_limit_bytes=8 << 20),
        name="query",
    )(trunk, gain, before, after, w_query)


def attend_kernel(head_dim, first, *refs):
    q_ref, rim_ref, refs = refs[0], refs[1], refs[2:]
    num_ref, den_ref = refs[-2:]
    pieces = refs[:-2] if first else refs[:-4]
    f32, bf16 = jnp.float32, jnp.bfloat16
    heads = q_ref.shape[1] // head_dim
    queries = jnp.concatenate(
        [q_ref[:, h * head_dim : (h + 1) * head_dim] for h in range(heads)] + [rim_ref[...]], 0
    )
    inner = 1.0 / (math.sqrt(head_dim) * logit_cap)
    outer = logit_cap * math.log2(math.e)
    num = jnp.zeros(num_ref.shape, f32) if first else refs[-4][...]
    den = jnp.zeros(den_ref.shape, f32) if first else refs[-3][...]
    step = 256
    for piece in pieces:
        for start in range(0, piece.shape[0], step):
            keys = piece[start : start + step, :head_dim]
            values = piece[start : start + step, head_dim:]
            scores = lax.dot_general(
                queries, keys, (((1,), (1,)), ((), ())), preferred_element_type=f32
            )
            weights = jnp.exp2(outer * jnp.tanh(scores * inner))
            num = num + jnp.dot(weights.astype(bf16), values, preferred_element_type=f32)
            for lane in range(0, step, 128):
                den = den + weights[:, lane : lane + 128]
    num_ref[...] = num
    den_ref[...] = den


def attend(state, queries, pieces, head_dim):
    rows = queries[0].size // head_dim + queries[1].shape[0]
    operands = [*queries, *pieces, *(state or ())]
    keys = sum(piece.shape[0] for piece in pieces)
    return pl.pallas_call(
        functools.partial(attend_kernel, head_dim, state is None),
        grid=(1,),
        in_specs=[whole(operand) for operand in operands],
        out_specs=[pl.BlockSpec((rows, head_dim), lambda i: (0, 0))] * 2,
        out_shape=[jax.ShapeDtypeStruct((rows, head_dim), jnp.float32)] * 2,
        cost_estimate=pl.CostEstimate(
            flops=8 * rows * keys * head_dim,
            transcendentals=2 * rows * keys,
            bytes_accessed=1 << 20,
        ),
        compiler_params=pltpu.CompilerParams(vmem_limit_bytes=8 << 20),
        name="attend",
    )(*operands)


def finish_kernel(
    at_ref, num_ref, den_ref, trunk_ref, before_ref, after_ref, out_ref, up_ref, skip_ref, conv_ref,
    feature_ref, ratio, near,
):
    f32, bf16 = jnp.float32, jnp.bfloat16
    rows, positions = trunk_ref.shape[0], skip_ref.shape[0]
    width, channels = trunk_ref.shape[1], skip_ref.shape[1]
    taps = conv_ref.shape[0]
    rim = taps // 2
    ratio[...] = num_ref[...] / jnp.sum(den_ref[...], axis=1, keepdims=True)
    heads = (ratio.shape[0] - 16) // rows
    attended = jnp.concatenate([ratio[h * rows : (h + 1) * rows, :] for h in range(heads)], 1)
    edge = jnp.concatenate(
        [ratio[heads * rows + 2 * h : heads * rows + 2 * h + 2, :] for h in range(heads)], 1
    )
    edge = jnp.concatenate([edge, jnp.zeros((14, edge.shape[1]), f32)], 0)
    attended = jnp.concatenate([attended.astype(bf16), edge.astype(bf16)], 0)
    sides = [
        jnp.concatenate(
            [ref[piece : piece + 1, :] for piece in range(width // channels)], 1
        ).astype(f32)
        for ref in (before_ref, after_ref)
    ]
    residual = jnp.concatenate(
        [trunk_ref[...].astype(f32)] + sides + [jnp.zeros((14, width), f32)], 0
    )
    hidden = (residual + jnp.dot(attended, out_ref[...], preferred_element_type=f32)).astype(bf16)
    upward = jnp.dot(hidden, up_ref[...], preferred_element_type=f32)
    factor = positions // rows
    for row in range(rows):
        begin = 8 + row * factor
        near[begin : begin + factor, :] = jnp.broadcast_to(
            upward[row : row + 1, :], (factor, channels)
        )
    inside = near[8 : 8 + positions, :] + skip_ref[...].astype(f32)
    near[8 : 8 + positions, :] = inside.astype(bf16).astype(f32)
    for index, (ref, begin) in enumerate(((before_ref, 8 - rim), (after_ref, 8 + positions))):
        tall = upward[rows + index : rows + index + 1, :] + ref[rim : 2 * rim, :].astype(f32)
        tall = tall.astype(bf16).astype(f32)
        near[begin : begin + rim, :] = jnp.where(at_ref[index] > 0, tall, 0.0)
    conved = jnp.zeros((positions, channels), f32)
    for tap in range(taps):
        begin = 8 - rim + tap
        conved = conved + jnp.dot(
            near[begin : begin + positions, :].astype(bf16),
            conv_ref[tap],
            preferred_element_type=f32,
        )
    cubic = math.sqrt(2.0 / math.pi) * (conved + 0.044715 * (conved * conved * conved))
    center = near[8 : 8 + positions, :]
    feature_ref[...] = (center + 0.5 * conved * (1.0 + jnp.tanh(cubic))).astype(bf16)


def finish(at, state, trunk, before, after, w_out, w_up, skip, conv_w):
    operands = (*state, trunk, before, after, w_out, w_up, skip, conv_w)
    vmem = pl.BlockSpec(memory_space=pltpu.VMEM)
    return pl.pallas_call(
        finish_kernel,
        in_specs=[pl.BlockSpec(memory_space=pltpu.SMEM)] + [vmem] * len(operands),
        out_specs=vmem,
        out_shape=jax.ShapeDtypeStruct(skip.shape, jnp.bfloat16),
        scratch_shapes=[
            pltpu.VMEM(state[0].shape, jnp.float32),
            pltpu.VMEM((skip.shape[0] + 16, skip.shape[1]), jnp.float32),
        ],
        cost_estimate=pl.CostEstimate(
            flops=2 * trunk.shape[0] * (w_out.size + w_up.size) + 2 * skip.shape[0] * conv_w.size,
            transcendentals=skip.size,
            bytes_accessed=2 * (w_out.size + w_up.size + conv_w.size),
        ),
        compiler_params=pltpu.CompilerParams(vmem_limit_bytes=14 << 20),
        name="finish",
    )(at, *operands)


def head_kernel(
    groups, first, last, positions, at_ref, *refs,
):
    f32, bf16 = jnp.float32, jnp.bfloat16
    halves, refs = refs[: 2 * groups], refs[2 * groups :]
    head_ref, bias_ref, scale_ref, keep_ref, target_ref = refs[:5]
    refs = refs[5:]
    if not first:
        old_ref, refs = refs[1], refs[2:]
    pred_ref, partials, sums = refs[0], refs[1 : 1 + groups], refs[1 + groups :]
    total_ref = sums[-1]
    step = pl.program_id(0)
    rows, channels = partials[0].shape
    bins = keep_ref.shape[2]
    factor = rows // bins
    row = lax.broadcasted_iota(jnp.int32, (rows, bins), 0)
    col = lax.broadcasted_iota(jnp.int32, (rows, bins), 1) * factor
    spread = jnp.where((row >= col) & (row < col + factor), 1.0, 0.0).astype(bf16)
    keep = lax.dot_general(
        spread,
        jnp.broadcast_to(keep_ref[0].astype(bf16), (8, bins)),
        (((1,), (1,)), ((), ())),
        preferred_element_type=f32,
    )[:, :1]
    feature = halves[-1][...]
    for index in range(len(halves) - 1):
        feature = jnp.where(step == index, halves[index][...], feature)
    logits = jnp.dot(feature, head_ref[...], preferred_element_type=f32) + bias_ref[...]
    decay = jnp.exp(-jnp.abs(logits))
    smooth = jnp.maximum(logits, 0.0) + jnp.log1p(decay)
    sigmoid = jnp.where(logits >= 0.0, 1.0, decay) / (1.0 + decay)
    pred_ref[...] = smooth.astype(bf16)
    misfit = smooth - target_ref[...].astype(f32)
    slope = (keep * scale_ref[...] * misfit * sigmoid).astype(bf16)
    partial = lax.dot_general(
        slope, head_ref[...], (((1,), (1,)), ((), ())), preferred_element_type=f32
    ).astype(bf16)
    for group in range(groups):

        @pl.when(lax.div(step, 2) == group)
        def _(group=group):
            partials[group][...] = partial

    product = lax.dot_general(
        feature, slope, (((0,), (0,)), ((), ())), preferred_element_type=f32
    )

    @pl.when(step == 0)
    def _():
        total_ref[...] = product if first else product + old_ref[...]

    @pl.when(step > 0)
    def _():
        total_ref[...] += product

    @pl.when(step == 2 * groups - 1)
    def _():
        if not last:
            return
        mine_ref, theirs_ref = sums[:2]
        core, height = at_ref[0], channels // 16
        for pair in range(8):
            at = pl.multiple_of((2 * pair + core) * height, height)
            other = pl.multiple_of((2 * pair + 1 - core) * height, height)
            into = slice(pair * height, (pair + 1) * height)
            mine_ref[into, :] = total_ref[pl.ds(at, height), :] / positions
            theirs_ref[into, :] = (total_ref[pl.ds(other, height), :] / positions).astype(bf16)


def head_pass(groups, at, carried, feature, head_w, bias, scale, keep, targets, last, positions):
    f32, bf16 = jnp.float32, jnp.bfloat16
    count, tracks = targets.shape
    channels = head_w.shape[0]
    rows = count // 8
    first = carried is None

    def segment(i, at):
        return at[2 + i // 2] * 2 + jnp.abs(at[1] - i % 2)

    by_rows = pl.BlockSpec((rows, tracks), lambda i, at: (segment(i, at), 0))
    by_group = [
        pl.BlockSpec((rows, channels), lambda i, at, g=g: (jnp.clip(i - 2 * g, 0, 1), 0))
        for g in range(groups)
    ]
    vmem = pl.BlockSpec(memory_space=pltpu.VMEM)
    totals = jax.ShapeDtypeStruct((channels, tracks), f32)
    half = (channels // 2, tracks)
    sums = [jax.ShapeDtypeStruct(half, f32), jax.ShapeDtypeStruct(half, bf16)] if last else [totals]
    return pl.pallas_call(
        functools.partial(head_kernel, groups, first, last, positions),
        grid_spec=pltpu.PrefetchScalarGridSpec(
            num_scalar_prefetch=1,
            grid=(2 * groups,),
            in_specs=[vmem] * (2 * groups + 3)
            + [pl.BlockSpec((1,) + keep.shape[1:], lambda i, at: (segment(i, at), 0, 0)), by_rows]
            + ([] if first else [pl.BlockSpec(memory_space=pl.ANY), vmem]),
            out_specs=[by_rows] + by_group + [vmem] * len(sums),
            scratch_shapes=[pltpu.VMEM((channels, tracks), f32)] if last else [],
        ),
        out_shape=[
            pltpu.HBM((count, tracks), bf16),
            *[jax.ShapeDtypeStruct((2 * rows, channels), bf16)] * groups,
            *sums,
        ],
        input_output_aliases={} if first else {6 + 2 * groups: 0},
        cost_estimate=pl.CostEstimate(
            flops=12 * groups * rows * head_w.size,
            transcendentals=8 * groups * rows * tracks,
            bytes_accessed=6 << 20,
        ),
        compiler_params=pltpu.CompilerParams(vmem_limit_bytes=16 << 20),
        name="head_pass",
    )(at, *feature, head_w, bias, scale, keep, targets, *(carried or ()))


def body(
    trunk,
    norm_gain,
    w_query,
    w_kv,
    w_out,
    w_up,
    skip,
    conv_w,
    head_w,
    head_bias,
    targets,
    missing,
    group_ids,
    group_weight,
):
    f32, bf16 = jnp.float32, jnp.bfloat16
    row_count = trunk.shape[0]
    head_dim = w_kv.shape[1] // 2
    head_count = w_query.shape[1] // head_dim
    n_all, index = lax.axis_size(ALL), lax.axis_index(ALL)
    channels = conv_w.shape[1]
    gain = norm_gain
    keyvals, to_next, to_prev = start(
        *[pltpu.with_memory_space_constraint(value, pltpu.HBM) for value in (trunk, gain, w_kv, skip)]
    )
    nexts = [(i, i + 1) for i in range(n_all - 1)]
    keyvals = join(keyvals, *[moved(keyvals, 2, step) for step in (1, 3, 2)])
    before = lax.ppermute(to_next, ALL, nexts)
    after = lax.ppermute(to_prev, ALL, [(j, i) for i, j in nexts])
    keyvals = join(keyvals, *[moved(keyvals, 1, step) for step in (1, 3, 2)])
    crossed = moved(keyvals, 3, 1)
    pieces = [moved(keyvals, 0, step) for step in (1, 3, 2)]
    pieces[0], before, after = lax.optimization_barrier((pieces[0], before, after))
    queries = query(trunk, gain, before, after, w_query, head_dim)
    pieces[1], queries = lax.optimization_barrier((pieces[1], queries))
    state = attend(None, queries, [keyvals], head_dim)
    for piece in pieces:
        state = attend(state, queries, [crossed, piece], head_dim)
        crossed = moved(piece, 3, 1)
    state = attend(state, queries, [crossed], head_dim)
    at = jnp.stack([index, n_all - 1 - index]).astype(jnp.int32)
    feature = finish(at, state, trunk, before, after, w_out, w_up, skip, conv_w)
    pos_count = targets.shape[0]
    n_bin = lax.axis_size(BIN)
    features = {0: (feature, moved(feature, 2, 2))}
    for step in (2, 1, 3):
        near = moved(feature, 1, step)
        features[step] = (near, moved(near, 2, 2))
    y, zh, core = lax.axis_index("y"), lax.axis_index("zh"), lax.axis_index("core")
    tile_width = head_w.shape[1]
    groups = group_weight.shape[0]
    total_tracks = group_ids.shape[0]
    labels = jnp.arange(groups, dtype=jnp.int32)
    counts = jnp.sum((group_ids == labels[None, :]).astype(jnp.int32), axis=0)
    per_group = group_weight * total_tracks / (groups * counts.astype(f32))
    local_ids = lax.dynamic_slice_in_dim(group_ids, lax.axis_index(TRK) * tile_width, tile_width, 0)
    track_scale = jnp.sum(jnp.where(local_ids == labels[None, :], per_group[None, :], 0.0), axis=1)
    keep_mask = 1.0 - missing.astype(f32).reshape(8, 1, missing.shape[0] // 8)
    targets = pltpu.with_memory_space_constraint(targets, pltpu.HBM)
    bias = head_bias[None, :]
    bias, far = lax.optimization_barrier((bias, features[0][1]))
    features[0] = (features[0][0], far)
    carried, received = None, {}
    for steps in ORDER:
        if 0 in steps:
            bias, received[2] = lax.optimization_barrier((bias, received[2]))
        prediction, *results = head_pass(
            len(steps),
            jnp.stack([core, zh] + [lax.rem(y + 4 - step, 4) for step in steps]).astype(jnp.int32),
            carried,
            [half for step in steps for half in features[step]],
            head_w,
            bias,
            track_scale[None, :],
            keep_mask,
            targets,
            0 in steps,
            pos_count * n_bin,
        )
        total = results[len(steps) :]
        carried = (prediction, *total)
        for step, partial in zip(steps, results):
            received[step] = moved(partial, 1, 4 - step) if step else partial
    mine, theirs = total
    theirs, received[1] = lax.optimization_barrier((theirs, received[1]))
    summed = sum(part.astype(f32) for part in received.values())
    half = summed.shape[0] // 2
    away = summed[half:].astype(bf16)
    feature_grad = (summed[:half] + moved(away, 2, 2).astype(f32)).astype(bf16)
    pair_sum = (mine + lax.ppermute(theirs, "core", [(0, 1), (1, 0)]).astype(f32)).astype(bf16)
    pair_sum = pair_sum.reshape(lax.axis_size("bz"), channels // n_bin, tile_width)
    gathered = lax.all_to_all(pair_sum, "bz", 0, 0, tiled=True)
    head_grad = jnp.sum(gathered.astype(f32), axis=0)
    return (prediction, head_grad, feature_grad)


def solution(mesh):
    inner = Mesh(np.asarray(mesh.devices).reshape(8, 2, 4, 2), ALL)
    in_specs = (
        P(ALL, None),
        P(),
        P(),
        P(),
        P(),
        P(),
        P(ALL, None),
        P(),
        P(None, TRK),
        P(TRK),
        P(BIN, TRK),
        P(BIN),
        P(),
        P(),
    )
    out_specs = (P(BIN, TRK), P(BIN, TRK), P(ALL, None))
    return jax.shard_map(body, mesh=inner, in_specs=in_specs, out_specs=out_specs, check_vma=False)
```

```python
import functools
import math

import jax
import jax.numpy as jnp
import numpy as np
from jax import lax
from jax.experimental import pallas as pl
from jax.experimental.pallas import tpu as pltpu
from jax.sharding import Mesh, PartitionSpec as P

logit_cap = 20.0
ORDER = ((2,), (1,), (3,), (0,))
BIN = ("bz", "core")
TRK = ("y", "zh")
ALL = BIN + TRK


def place(index):
    bz, rest = divmod(index, 16)
    core, rest = divmod(rest, 8)
    y, zh = divmod(rest, 2)
    zlo, x = divmod(bz, 4)
    return (x, y, zh * 2 + zlo, core)


def number(x, y, z, core):
    zh, zlo = divmod(z, 2)
    return ((zlo * 4 + x) * 2 + core) * 8 + y * 2 + zh


def moved(value, dim, step):
    sizes = (4, 4, 4, 2)
    pairs = []
    for index in range(128):
        target = list(place(index))
        target[dim] = (target[dim] + step) % sizes[dim]
        pairs.append((index, number(*target)))
    return lax.ppermute(value, ALL, pairs)


def whole(array):
    return pl.BlockSpec(array.shape, lambda *_: (0,) * array.ndim, pipeline_mode=pl.Buffered(1))


def join_kernel(*refs):
    out = refs[-1]
    rows = refs[0].shape[0]
    for index, ref in enumerate(refs[:-1]):
        out[index * rows : (index + 1) * rows, :] = ref[...]


def join(*pieces):
    rows, columns = pieces[0].shape
    out = jax.ShapeDtypeStruct((len(pieces) * rows, columns), pieces[0].dtype)
    return pl.pallas_call(
        join_kernel,
        in_specs=[pl.BlockSpec(memory_space=pltpu.VMEM)] * len(pieces),
        out_specs=pl.BlockSpec(memory_space=pltpu.VMEM),
        out_shape=out,
        cost_estimate=pl.CostEstimate(flops=0, transcendentals=0, bytes_accessed=4 * out.size),
        compiler_params=pltpu.CompilerParams(vmem_limit_bytes=4 << 20),
        name="join",
    )(*pieces)


def normalized(value, gain):
    widened = value.astype(jnp.float32)
    meansq = jnp.mean(widened * widened, axis=1, keepdims=True)
    return (widened * lax.rsqrt(meansq + 1e-06) * gain).astype(jnp.bfloat16)


def start_kernel(trunk_ref, gain_ref, kv_ref, skip_ref, keyvals_ref, next_ref, prev_ref, tall):
    f32, bf16 = jnp.float32, jnp.bfloat16
    normed = normalized(trunk_ref[...], gain_ref[...])
    keyvals_ref[...] = jnp.dot(normed, kv_ref[...], preferred_element_type=f32).astype(bf16)
    rows, width = trunk_ref.shape
    positions, channels = skip_ref.shape
    count = width // channels
    widened = trunk_ref[...].astype(f32)
    for out, row, near in ((next_ref, rows - 1, positions - 8), (prev_ref, 0, 0)):
        tall[...] = skip_ref[near : near + 8, :].astype(f32)
        rim = tall[6:8, :] if row else tall[0:2, :]
        tall[count : count + 2, :] = rim
        for piece in range(count):
            tall[piece : piece + 1, :] = widened[
                row : row + 1, piece * channels : (piece + 1) * channels
            ]
        out[...] = tall[...].astype(bf16)


def start(trunk, gain, w_kv, skip):
    vmem = pl.BlockSpec(memory_space=pltpu.VMEM)
    edge = jax.ShapeDtypeStruct((8, skip.shape[1]), jnp.bfloat16)
    return pl.pallas_call(
        start_kernel,
        grid=(1,),
        in_specs=[whole(operand) for operand in (trunk, gain, w_kv, skip)],
        out_specs=[vmem] * 3,
        out_shape=[jax.ShapeDtypeStruct((trunk.shape[0], w_kv.shape[1]), jnp.bfloat16), edge, edge],
        scratch_shapes=[pltpu.VMEM(edge.shape, jnp.float32)],
        cost_estimate=pl.CostEstimate(
            flops=2 * trunk.shape[0] * w_kv.size, transcendentals=64, bytes_accessed=2 * w_kv.size
        ),
        compiler_params=pltpu.CompilerParams(vmem_limit_bytes=6 << 20),
        name="start",
    )(trunk, gain, w_kv, skip)


def query_kernel(trunk_ref, gain_ref, before_ref, after_ref, w_ref, queries_ref, rims_ref, tall):
    f32, bf16 = jnp.float32, jnp.bfloat16
    rows, width = trunk_ref.shape
    channels, head_dim = before_ref.shape[1], rims_ref.shape[1]
    sides = [
        jnp.concatenate(
            [ref[piece : piece + 1, :].astype(f32) for piece in range(width // channels)], 1
        )
        for ref in (before_ref, after_ref)
    ]
    every = jnp.concatenate(
        [trunk_ref[...].astype(f32)] + sides + [jnp.zeros((14, width), f32)], 0
    )
    normed = normalized(every, gain_ref[...])
    projected = jnp.dot(normed, w_ref[...], preferred_element_type=f32)
    queries_ref[...] = projected[:rows].astype(bf16)
    for head in range(projected.shape[1] // head_dim):
        tall[2 * head : 2 * head + 2, :] = projected[
            rows : rows + 2, head * head_dim : (head + 1) * head_dim
        ]
    rims_ref[...] = tall[...].astype(bf16)


def query(trunk, gain, before, after, w_query, head_dim):
    vmem = pl.BlockSpec(memory_space=pltpu.VMEM)
    rims = (2 * w_query.shape[1] // head_dim, head_dim)
    return pl.pallas_call(
        query_kernel,
        in_specs=[vmem] * 5,
        out_specs=[vmem] * 2,
        out_shape=[
            jax.ShapeDtypeStruct((trunk.shape[0], w_query.shape[1]), jnp.bfloat16),
            jax.ShapeDtypeStruct(rims, jnp.bfloat16),
        ],
        scratch_shapes=[pltpu.VMEM(rims, jnp.float32)],
        cost_estimate=pl.CostEstimate(
            flops=2 * trunk.shape[0] * w_query.size,
            transcendentals=64,
            bytes_accessed=2 * w_query.size,
        ),
        compiler_params=pltpu.CompilerParams(vmem_limit_bytes=8 << 20),
        name="query",
    )(trunk, gain, before, after, w_query)


def attend_kernel(head_dim, first, *refs):
    q_ref, rim_ref, refs = refs[0], refs[1], refs[2:]
    num_ref, den_ref = refs[-2:]
    pieces = refs[:-2] if first else refs[:-4]
    f32, bf16 = jnp.float32, jnp.bfloat16
    heads = q_ref.shape[1] // head_dim
    queries = jnp.concatenate(
        [q_ref[:, h * head_dim : (h + 1) * head_dim] for h in range(heads)] + [rim_ref[...]], 0
    )
    inner = 1.0 / (math.sqrt(head_dim) * logit_cap)
    outer = logit_cap * math.log2(math.e)
    num = jnp.zeros(num_ref.shape, f32) if first else refs[-4][...]
    den = jnp.zeros(den_ref.shape, f32) if first else refs[-3][...]
    step = 256
    for piece in pieces:
        for start in range(0, piece.shape[0], step):
            keys = piece[start : start + step, :head_dim]
            values = piece[start : start + step, head_dim:]
            scores = lax.dot_general(
                queries, keys, (((1,), (1,)), ((), ())), preferred_element_type=f32
            )
            weights = jnp.exp2(outer * jnp.tanh(scores * inner))
            num = num + jnp.dot(weights.astype(bf16), values, preferred_element_type=f32)
            for lane in range(0, step, 128):
                den = den + weights[:, lane : lane + 128]
    num_ref[...] = num
    den_ref[...] = den


def attend(state, queries, pieces, head_dim):
    rows = queries[0].size // head_dim + queries[1].shape[0]
    operands = [*queries, *pieces, *(state or ())]
    keys = sum(piece.shape[0] for piece in pieces)
    return pl.pallas_call(
        functools.partial(attend_kernel, head_dim, state is None),
        grid=(1,),
        in_specs=[whole(operand) for operand in operands],
        out_specs=[pl.BlockSpec((rows, head_dim), lambda i: (0, 0))] * 2,
        out_shape=[jax.ShapeDtypeStruct((rows, head_dim), jnp.float32)] * 2,
        cost_estimate=pl.CostEstimate(
            flops=8 * rows * keys * head_dim,
            transcendentals=2 * rows * keys,
            bytes_accessed=1 << 20,
        ),
        compiler_params=pltpu.CompilerParams(vmem_limit_bytes=8 << 20),
        name="attend",
    )(*operands)


def finish_kernel(
    at_ref, num_ref, den_ref, trunk_ref, before_ref, after_ref, out_ref, up_ref, skip_ref, conv_ref,
    feature_ref, ratio, near,
):
    f32, bf16 = jnp.float32, jnp.bfloat16
    rows, positions = trunk_ref.shape[0], skip_ref.shape[0]
    width, channels = trunk_ref.shape[1], skip_ref.shape[1]
    taps = conv_ref.shape[0]
    rim = taps // 2
    ratio[...] = num_ref[...] / jnp.sum(den_ref[...], axis=1, keepdims=True)
    heads = (ratio.shape[0] - 16) // rows
    attended = jnp.concatenate([ratio[h * rows : (h + 1) * rows, :] for h in range(heads)], 1)
    edge = jnp.concatenate(
        [ratio[heads * rows + 2 * h : heads * rows + 2 * h + 2, :] for h in range(heads)], 1
    )
    edge = jnp.concatenate([edge, jnp.zeros((14, edge.shape[1]), f32)], 0)
    attended = jnp.concatenate([attended.astype(bf16), edge.astype(bf16)], 0)
    sides = [
        jnp.concatenate(
            [ref[piece : piece + 1, :] for piece in range(width // channels)], 1
        ).astype(f32)
        for ref in (before_ref, after_ref)
    ]
    residual = jnp.concatenate(
        [trunk_ref[...].astype(f32)] + sides + [jnp.zeros((14, width), f32)], 0
    )
    hidden = (residual + jnp.dot(attended, out_ref[...], preferred_element_type=f32)).astype(bf16)
    upward = jnp.dot(hidden, up_ref[...], preferred_element_type=f32)
    factor = positions // rows
    for row in range(rows):
        begin = 8 + row * factor
        near[begin : begin + factor, :] = jnp.broadcast_to(
            upward[row : row + 1, :], (factor, channels)
        )
    inside = near[8 : 8 + positions, :] + skip_ref[...].astype(f32)
    near[8 : 8 + positions, :] = inside.astype(bf16).astype(f32)
    for index, (ref, begin) in enumerate(((before_ref, 8 - rim), (after_ref, 8 + positions))):
        tall = upward[rows + index : rows + index + 1, :] + ref[rim : 2 * rim, :].astype(f32)
        tall = tall.astype(bf16).astype(f32)
        near[begin : begin + rim, :] = jnp.where(at_ref[index] > 0, tall, 0.0)
    conved = jnp.zeros((positions, channels), f32)
    for tap in range(taps):
        begin = 8 - rim + tap
        conved = conved + jnp.dot(
            near[begin : begin + positions, :].astype(bf16),
            conv_ref[tap],
            preferred_element_type=f32,
        )
    cubic = math.sqrt(2.0 / math.pi) * (conved + 0.044715 * (conved * conved * conved))
    center = near[8 : 8 + positions, :]
    feature_ref[...] = (center + 0.5 * conved * (1.0 + jnp.tanh(cubic))).astype(bf16)


def finish(at, state, trunk, before, after, w_out, w_up, skip, conv_w):
    operands = (*state, trunk, before, after, w_out, w_up, skip, conv_w)
    vmem = pl.BlockSpec(memory_space=pltpu.VMEM)
    return pl.pallas_call(
        finish_kernel,
        in_specs=[pl.BlockSpec(memory_space=pltpu.SMEM)] + [vmem] * len(operands),
        out_specs=vmem,
        out_shape=jax.ShapeDtypeStruct(skip.shape, jnp.bfloat16),
        scratch_shapes=[
            pltpu.VMEM(state[0].shape, jnp.float32),
            pltpu.VMEM((skip.shape[0] + 16, skip.shape[1]), jnp.float32),
        ],
        cost_estimate=pl.CostEstimate(
            flops=2 * trunk.shape[0] * (w_out.size + w_up.size) + 2 * skip.shape[0] * conv_w.size,
            transcendentals=skip.size,
            bytes_accessed=2 * (w_out.size + w_up.size + conv_w.size),
        ),
        compiler_params=pltpu.CompilerParams(vmem_limit_bytes=14 << 20),
        name="finish",
    )(at, *operands)


def head_kernel(
    groups, first, last, positions, at_ref, *refs,
):
    f32, bf16 = jnp.float32, jnp.bfloat16
    halves, refs = refs[: 2 * groups], refs[2 * groups :]
    head_ref, bias_ref, scale_ref, keep_ref, target_ref = refs[:5]
    refs = refs[5:]
    if not first:
        old_ref, refs = refs[1], refs[2:]
    pred_ref, partials, sums = refs[0], refs[1 : 1 + groups], refs[1 + groups :]
    total_ref = sums[-1]
    step = pl.program_id(0)
    rows, channels = partials[0].shape
    bins = keep_ref.shape[2]
    factor = rows // bins
    row = lax.broadcasted_iota(jnp.int32, (rows, bins), 0)
    col = lax.broadcasted_iota(jnp.int32, (rows, bins), 1) * factor
    spread = jnp.where((row >= col) & (row < col + factor), 1.0, 0.0).astype(bf16)
    keep = lax.dot_general(
        spread,
        jnp.broadcast_to(keep_ref[0].astype(bf16), (8, bins)),
        (((1,), (1,)), ((), ())),
        preferred_element_type=f32,
    )[:, :1]
    feature = halves[-1][...]
    for index in range(len(halves) - 1):
        feature = jnp.where(step == index, halves[index][...], feature)
    logits = jnp.dot(feature, head_ref[...], preferred_element_type=f32) + bias_ref[...]
    decay = jnp.exp(-jnp.abs(logits))
    smooth = jnp.maximum(logits, 0.0) + jnp.log1p(decay)
    sigmoid = jnp.where(logits >= 0.0, 1.0, decay) / (1.0 + decay)
    pred_ref[...] = smooth.astype(bf16)
    misfit = smooth - target_ref[...].astype(f32)
    slope = (keep * scale_ref[...] * misfit * sigmoid).astype(bf16)
    partial = lax.dot_general(
        slope, head_ref[...], (((1,), (1,)), ((), ())), preferred_element_type=f32
    ).astype(bf16)
    for group in range(groups):

        @pl.when(lax.div(step, 2) == group)
        def _(group=group):
            partials[group][...] = partial

    product = lax.dot_general(
        feature, slope, (((0,), (0,)), ((), ())), preferred_element_type=f32
    )

    @pl.when(step == 0)
    def _():
        total_ref[...] = product if first else product + old_ref[...]

    @pl.when(step > 0)
    def _():
        total_ref[...] += product

    @pl.when(step == 2 * groups - 1)
    def _():
        if not last:
            return
        mine_ref, theirs_ref = sums[:2]
        core, height = at_ref[0], channels // 16
        for pair in range(8):
            at = pl.multiple_of((2 * pair + core) * height, height)
            other = pl.multiple_of((2 * pair + 1 - core) * height, height)
            into = slice(pair * height, (pair + 1) * height)
            mine_ref[into, :] = total_ref[pl.ds(at, height), :] / positions
            theirs_ref[into, :] = (total_ref[pl.ds(other, height), :] / positions).astype(bf16)


def head_pass(groups, at, carried, feature, head_w, bias, scale, keep, targets, last, positions):
    f32, bf16 = jnp.float32, jnp.bfloat16
    count, tracks = targets.shape
    channels = head_w.shape[0]
    rows = count // 8
    first = carried is None

    def segment(i, at):
        return at[2 + i // 2] * 2 + jnp.abs(at[1] - i % 2)

    by_rows = pl.BlockSpec((rows, tracks), lambda i, at: (segment(i, at), 0))
    by_group = [
        pl.BlockSpec((rows, channels), lambda i, at, g=g: (jnp.clip(i - 2 * g, 0, 1), 0))
        for g in range(groups)
    ]
    vmem = pl.BlockSpec(memory_space=pltpu.VMEM)
    totals = jax.ShapeDtypeStruct((channels, tracks), f32)
    half = (channels // 2, tracks)
    sums = [jax.ShapeDtypeStruct(half, f32), jax.ShapeDtypeStruct(half, bf16)] if last else [totals]
    return pl.pallas_call(
        functools.partial(head_kernel, groups, first, last, positions),
        grid_spec=pltpu.PrefetchScalarGridSpec(
            num_scalar_prefetch=1,
            grid=(2 * groups,),
            in_specs=[vmem] * (2 * groups + 3)
            + [pl.BlockSpec((1,) + keep.shape[1:], lambda i, at: (segment(i, at), 0, 0)), by_rows]
            + ([] if first else [pl.BlockSpec(memory_space=pl.ANY), vmem]),
            out_specs=[by_rows] + by_group + [vmem] * len(sums),
            scratch_shapes=[pltpu.VMEM((channels, tracks), f32)] if last else [],
        ),
        out_shape=[
            pltpu.HBM((count, tracks), bf16),
            *[jax.ShapeDtypeStruct((2 * rows, channels), bf16)] * groups,
            *sums,
        ],
        input_output_aliases={} if first else {6 + 2 * groups: 0},
        cost_estimate=pl.CostEstimate(
            flops=12 * groups * rows * head_w.size,
            transcendentals=8 * groups * rows * tracks,
            bytes_accessed=6 << 20,
        ),
        compiler_params=pltpu.CompilerParams(vmem_limit_bytes=16 << 20),
        name="head_pass",
    )(at, *feature, head_w, bias, scale, keep, targets, *(carried or ()))


def body(
    trunk,
    norm_gain,
    w_query,
    w_kv,
    w_out,
    w_up,
    skip,
    conv_w,
    head_w,
    head_bias,
    targets,
    missing,
    group_ids,
    group_weight,
):
    f32, bf16 = jnp.float32, jnp.bfloat16
    row_count = trunk.shape[0]
    head_dim = w_kv.shape[1] // 2
    head_count = w_query.shape[1] // head_dim
    n_all, index = lax.axis_size(ALL), lax.axis_index(ALL)
    channels = conv_w.shape[1]
    gain = norm_gain
    keyvals, to_next, to_prev = start(
        *[pltpu.with_memory_space_constraint(value, pltpu.HBM) for value in (trunk, gain, w_kv, skip)]
    )
    nexts = [(i, i + 1) for i in range(n_all - 1)]
    keyvals = join(keyvals, *[moved(keyvals, 2, step) for step in (1, 3, 2)])
    before = lax.ppermute(to_next, ALL, nexts)
    after = lax.ppermute(to_prev, ALL, [(j, i) for i, j in nexts])
    keyvals = join(keyvals, *[moved(keyvals, 1, step) for step in (1, 3, 2)])
    crossed = moved(keyvals, 3, 1)
    pieces = [moved(keyvals, 0, step) for step in (1, 3, 2)]
    pieces[0], before, after = lax.optimization_barrier((pieces[0], before, after))
    queries = query(trunk, gain, before, after, w_query, head_dim)
    pieces[1], queries = lax.optimization_barrier((pieces[1], queries))
    state = attend(None, queries, [keyvals], head_dim)
    for piece in pieces:
        state = attend(state, queries, [crossed, piece], head_dim)
        crossed = moved(piece, 3, 1)
    state = attend(state, queries, [crossed], head_dim)
    at = jnp.stack([index, n_all - 1 - index]).astype(jnp.int32)
    feature = finish(at, state, trunk, before, after, w_out, w_up, skip, conv_w)
    pos_count = targets.shape[0]
    n_bin = lax.axis_size(BIN)
    features = {0: (feature, moved(feature, 2, 2))}
    for step in (2, 1, 3):
        near = moved(feature, 1, step)
        features[step] = (near, moved(near, 2, 2))
    y, zh, core = lax.axis_index("y"), lax.axis_index("zh"), lax.axis_index("core")
    tile_width = head_w.shape[1]
    groups = group_weight.shape[0]
    total_tracks = group_ids.shape[0]
    labels = jnp.arange(groups, dtype=jnp.int32)
    counts = jnp.sum((group_ids == labels[None, :]).astype(jnp.int32), axis=0)
    per_group = group_weight * total_tracks / (groups * counts.astype(f32))
    local_ids = lax.dynamic_slice_in_dim(group_ids, lax.axis_index(TRK) * tile_width, tile_width, 0)
    track_scale = jnp.sum(jnp.where(local_ids == labels[None, :], per_group[None, :], 0.0), axis=1)
    keep_mask = 1.0 - missing.astype(f32).reshape(8, 1, missing.shape[0] // 8)
    targets = pltpu.with_memory_space_constraint(targets, pltpu.HBM)
    bias = head_bias[None, :]
    carried, received = None, {}
    for steps in ORDER:
        if 0 in steps:
            bias, received[2] = lax.optimization_barrier((bias, received[2]))
        prediction, *results = head_pass(
            len(steps),
            jnp.stack([core, zh] + [lax.rem(y + 4 - step, 4) for step in steps]).astype(jnp.int32),
            carried,
            [half for step in steps for half in features[step]],
            head_w,
            bias,
            track_scale[None, :],
            keep_mask,
            targets,
            0 in steps,
            pos_count * n_bin,
        )
        total = results[len(steps) :]
        carried = (prediction, *total)
        for step, partial in zip(steps, results):
            received[step] = moved(partial, 1, 4 - step) if step else partial
    mine, theirs = total
    summed = sum(part.astype(f32) for part in received.values())
    half = summed.shape[0] // 2
    away = summed[half:].astype(bf16)
    feature_grad = (summed[:half] + moved(away, 2, 2).astype(f32)).astype(bf16)
    pair_sum = (mine + lax.ppermute(theirs, "core", [(0, 1), (1, 0)]).astype(f32)).astype(bf16)
    pair_sum = pair_sum.reshape(lax.axis_size("bz"), channels // n_bin, tile_width)
    gathered = lax.all_to_all(pair_sum, "bz", 0, 0, tiled=True)
    head_grad = jnp.sum(gathered.astype(f32), axis=0)
    return (prediction, head_grad, feature_grad)


def solution(mesh):
    inner = Mesh(np.asarray(mesh.devices).reshape(8, 2, 4, 2), ALL)
    in_specs = (
        P(ALL, None),
        P(),
        P(),
        P(),
        P(),
        P(),
        P(ALL, None),
        P(),
        P(None, TRK),
        P(TRK),
        P(BIN, TRK),
        P(BIN),
        P(),
        P(),
    )
    out_specs = (P(BIN, TRK), P(BIN, TRK), P(ALL, None))
    return jax.shard_map(body, mesh=inner, in_specs=in_specs, out_specs=out_specs, check_vma=False)
```
